256 devices in a mesh: ia: 8 (over y_lo, x), ja: 4 (over y_hi, core), ka: 8 (over z).
Axes of the slice: x: 4, y: 4 (y_hi: 2, y_lo: 2; y = y_hi * 2 + y_lo), z: 8, core: 2. Of those that a mesh axis runs over, the one named last changes fastest.
Arguments:
- tensor: bfloat16 [2048, 512, 1024], P('ia', 'ja', 'ka'), may hold values from 0 to 122880
- matrix: bfloat16 [2048, 262144], P(None, ('ia', 'ja', 'ka')), may hold values from 0 to 1024000
- first_factor: bfloat16 [2048, 256], P('ia'), may hold values from 0.05 to 2
- second_factor: bfloat16 [512, 256], P('ja'), may hold values from 0.05 to 2
- time_factor: bfloat16 [1024, 256], P('ka'), may hold values from 0.05 to 2
- column_factor: bfloat16 [262144, 256], P(('ia', 'ja', 'ka')), may hold values from 0.05 to 2
Outputs:
- first_new: bfloat16 [2048, 256], P('ia')
- second_new: bfloat16 [512, 256], P('ja')
- time_new: bfloat16 [1024, 256], P('ka')
The draws below stay inside these ranges and needn't reach their ends.
All inputs are finite; a program needn't handle non-finite values.
Results may differ from the reference program's by a relative error of at most 0.00075.
The reference program's roundings to bfloat16 on the way (of `khatri`) count: a program that leaves them out, or rounds other values in their place, can miss the bound.
Values may be sent and summed in bfloat16 or wider, within the bound.
A program may use at most 128 MiB of HBM per device.

```python
import jax
import jax.numpy as jnp
from jax import lax

R = 256
I_DEV = 256
M_DEV = 1024
I = 2048
J = 512
K = 1024
M = 262144


component_count = 512


def drawn_members(key):
    member_key = jax.random.fold_in(key, 41)
    key_list = jax.random.split(member_key, 2)
    members = jax.random.randint(key_list[0], (I, 2), 0, component_count)
    weights = jnp.exp(jax.random.uniform(key_list[1], (I, 2), jnp.float32, -0.7, 0.7))
    return (members, weights)


def peaked_columns(key, length, fraction):
    key_list = jax.random.split(key, 2)
    support = (jax.random.uniform(key_list[0], (length, component_count), jnp.float32, 0.0, 1.0) < fraction).astype(jnp.float32)
    return support * jnp.exp(jax.random.uniform(key_list[1], (length, component_count), jnp.float32, -0.7, 0.7))


def draw_tensor(key, part):
    members, weights = drawn_members(key)
    key_list = jax.random.split(jax.random.fold_in(key, 3), 3)
    plane_columns = peaked_columns(key_list[0], J, 0.0625)
    time_columns = peaked_columns(key_list[1], K, 0.0625)
    plane_rows = plane_columns.T[members] * weights[:, :, None]
    time_rows = time_columns.T[members]
    planted = jnp.einsum('isj,isk->ijk', plane_rows, time_rows)
    noise = jax.random.uniform(key_list[2], (I, J, K), jnp.float32, 0.0, 1.0)
    mass = jnp.minimum(noise + 128.0 * planted, 960.0)
    return (0.5 * R * mass).astype(jnp.bfloat16)


def draw_matrix(key, part):
    key_list = jax.random.split(jax.random.fold_in(key, 5), 3)
    blocks_total = M // M_DEV
    row_span = I // blocks_total
    pairing = jax.random.permutation(key_list[0], blocks_total)
    row_owner = pairing[jnp.arange(I) // row_span]
    column_block = jnp.arange(M) // M_DEV
    paired = (row_owner[:, None] == column_block[None, :]).astype(jnp.float32)
    heavy = jnp.exp(3.5 * jax.random.normal(key_list[1], (I, M), jnp.float32))
    spread = jax.random.uniform(key_list[2], (I, M), jnp.float32, 0.5, 1.5)
    mass = heavy + paired * (48.0 * blocks_total) * spread
    size_scale = R * J * K / (100.0 * M)
    ceiling = 2000.0 * R * J * K / M
    return jnp.minimum(mass * size_scale, ceiling).astype(jnp.bfloat16)


def level_scale(key, row_count):
    levels = jax.random.uniform(key, (8, 8), jnp.float32, -1.1, 0.9)
    row_block = jnp.arange(row_count) * 8 // row_count
    rank_block = jnp.arange(R) * 8 // R
    return jnp.exp(levels[row_block][:, rank_block])


def level_factor(key, row_count):
    key_list = jax.random.split(key, 2)
    scale = level_scale(key_list[0], row_count)
    base = jax.random.uniform(key_list[1], (row_count, R), jnp.float32, 0.4, 1.4)
    return jnp.clip(base * scale, 0.05, 2.0).astype(jnp.bfloat16)


def draw_first_factor(key, part):
    return level_factor(jax.random.fold_in(key, 61), I)


def draw_second_factor(key, part):
    return level_factor(jax.random.fold_in(key, 67), J)


def draw_time_factor(key, part):
    return level_factor(jax.random.fold_in(key, 71), K)


def draw_column_factor(key, part):
    key_list = jax.random.split(jax.random.fold_in(key, 73), 2)
    scale = level_scale(key_list[0], M)
    base = jnp.exp(jax.random.uniform(key_list[1], (M, R), jnp.float32, -1.8971, 0.4055))
    return jnp.clip(base * scale, 0.05, 2.0).astype(jnp.bfloat16)


def setup_inputs(seed: int = 0) -> dict:
    streams_of = jax.random.split(jax.random.key(seed), 7)
    return {
        "tensor": draw_tensor(jax.random.fold_in(streams_of[6], 71), 0),
        "matrix": draw_matrix(jax.random.fold_in(streams_of[6], 71), 0),
        "first_factor": draw_first_factor(jax.random.fold_in(streams_of[6], 71), 0),
        "second_factor": draw_second_factor(jax.random.fold_in(streams_of[6], 71), 0),
        "time_factor": draw_time_factor(jax.random.fold_in(streams_of[6], 71), 0),
        "column_factor": draw_column_factor(jax.random.fold_in(streams_of[6], 71), 0),
    }


def cross_product(values):
    return jnp.dot(values.T, values, preferred_element_type=jnp.float32)


def rescale(factor, numerator, gram_total):
    widened = factor.astype(jnp.float32)
    denominator = jnp.dot(widened, gram_total, precision=lax.Precision.HIGHEST)
    return (widened * numerator / denominator).astype(jnp.bfloat16)


def reference(tensor, matrix, first_factor, second_factor, time_factor, column_factor):
    gram_second = cross_product(second_factor)
    gram_time = cross_product(time_factor)
    gram_column = cross_product(column_factor)
    khatri = (second_factor.astype(jnp.float32)[:, None, :] * time_factor.astype(jnp.float32)[None, :, :]).astype(jnp.bfloat16).reshape(J * K, R)
    blocked = tensor.reshape(I // I_DEV, I_DEV, J * K)

    def slab_block(tile_rows):
        return jnp.dot(tile_rows, khatri, preferred_element_type=jnp.float32)

    slab = lax.map(slab_block, blocked).reshape(I, R)

    def add_columns(step, total):
        start = (step * M_DEV).astype(jnp.int32)
        columns = lax.dynamic_slice_in_dim(matrix, start, M_DEV, 1)
        factor_rows = lax.dynamic_slice_in_dim(column_factor, start, M_DEV, 0)
        return total + jnp.dot(columns, factor_rows, preferred_element_type=jnp.float32)

    coupled = lax.fori_loop(0, M // M_DEV, add_columns, jnp.zeros((I, R), jnp.float32))
    first_new = rescale(first_factor, slab + coupled, gram_second * gram_time + gram_column)

    def add_weighted(step, total):
        start = (step * I_DEV).astype(jnp.int32)
        tile_rows = lax.dynamic_slice_in_dim(tensor, start, I_DEV, 0)
        factor_rows = lax.dynamic_slice_in_dim(first_new, start, I_DEV, 0)
        return total + lax.dot_general(tile_rows, factor_rows, (((0,), (0,)), ((), ())), preferred_element_type=jnp.float32)

    weighted = lax.fori_loop(0, I // I_DEV, add_weighted, jnp.zeros((J, K, R), jnp.float32))
    plane_sum = jnp.sum(weighted * time_factor.astype(jnp.float32)[None, :, :], axis=1)
    gram_first = cross_product(first_new)
    second_new = rescale(second_factor, plane_sum, gram_first * gram_time)
    time_sum = jnp.sum(weighted * second_new.astype(jnp.float32)[:, None, :], axis=0)
    gram_new = cross_product(second_new)
    time_new = rescale(time_factor, time_sum, gram_first * gram_new)
    return (first_new, second_new, time_new)
```

```python
import functools

import jax
import jax.numpy as jnp
from jax import lax
from jax.experimental import pallas as pl
from jax.experimental.pallas import tpu as pltpu
from jax.sharding import PartitionSpec as P

F32 = jnp.float32
BF16 = jnp.bfloat16


def dot(a, b):
    return jnp.dot(a, b, preferred_element_type=F32)


def dot_nt(a, b):
    return lax.dot_general(a, b, (((1,), (1,)), ((), ())), preferred_element_type=F32)


def identity(n):
    rows = lax.broadcasted_iota(jnp.int32, (n, n), 0)
    columns = lax.broadcasted_iota(jnp.int32, (n, n), 1)
    return (rows == columns).astype(F32).astype(BF16)


def transposed(values):
    return dot_nt(identity(values.shape[1]), values)


def exact_product(gram, factor):
    rows = gram.shape[0]
    high = gram.astype(BF16).astype(F32)
    rest = gram - high
    middle = rest.astype(BF16).astype(F32)
    low = (rest - middle).astype(BF16).astype(F32)
    parts = [high, middle, low]
    while (rows * len(parts)) % 16:
        parts.append(jnp.zeros_like(high))
    stacked = dot_nt(jnp.concatenate(parts, axis=0).astype(BF16), factor)
    return stacked[:rows] + (stacked[rows : 2 * rows] + stacked[2 * rows : 3 * rows])


def kernel(
    sizes,
    tensor_ref,
    matrix_ref,
    first_ref,
    second_ref,
    time_ref,
    column_ref,
    first_out,
    second_out,
    time_out,
    tens,
    perm,
    wide,
    mats,
    col_t,
    coup,
    pair_in,
    ring_in,
    slab_acc,
    slab_half,
    slab_in,
    sum_half,
    sum_in,
    gc_loc,
    gc_in,
    gs_loc,
    gs_in,
    gt_loc,
    gt_in,
    gt_sum,
    ga_in,
    first_t,
    second_t,
    time_t,
    second_f,
    time_f,
    fn_in,
    fn_rows,
    gf_loc,
    gfa_in,
    gfb_in,
    plane,
    ps_loc,
    ps_in,
    pa_in,
    sn_in,
    sn_groups,
    gn_loc,
    gn_in,
    tsum,
    ts_loc,
    ts_in,
    tn_in,
    mat_sem,
    tens_sem,
    pair_send,
    pair_recv,
    send_sem,
    recv_sem,
):
    nia, nja, nka, rank, ti, tj, tk = sizes
    nyh = nja // 2
    slots = nja * nka
    q1, q2, q3 = rank // slots, rank // nka, rank // (nia * nja)
    groups = nka * nyh
    half = tj // 2
    ia, ja, ka = lax.axis_index("ia"), lax.axis_index("ja"), lax.axis_index("ka")
    core = lax.rem(ja, 2)
    other = 1 - core
    yh = ja // 2
    slot1 = ka * nja + ja
    group = ka * nyh + yh
    slot3 = ia * nja + ja

    def wrap(value, n):
        return lax.rem(value + n, n)

    def remote(src, dst, s_sem, r_sem, dia, dja, dka):
        return pltpu.make_async_remote_copy(
            src_ref=src,
            dst_ref=dst,
            send_sem=s_sem,
            recv_sem=r_sem,
            device_id=(dia, dja, dka),
            device_id_type=pl.DeviceIdType.MESH,
        )

    def wait_bytes(ref, sem):
        pltpu.make_async_copy(ref, ref, sem).wait()

    def block_of(s):
        return wrap(ia + 1 + s, nia)

    def mat_copy(s):
        rows = pl.ds(pl.multiple_of(block_of(s) * ti, ti), ti)
        return pltpu.make_async_copy(matrix_ref.at[rows, :], mats.at[s], mat_sem.at[s])

    def tens_copy(b):
        rows = pl.ds(b * 16, 16)
        return pltpu.make_async_copy(tensor_ref.at[rows], tens.at[rows], tens_sem.at[b])

    @pl.loop(0, nia)
    def _(s):
        mat_copy(s).start()

    @pl.loop(0, ti // 16)
    def _(b):
        tens_copy(b).start()

    barrier = pltpu.get_barrier_semaphore()

    @pl.loop(1, slots)
    def _(t):
        pl.semaphore_signal(
            barrier,
            inc=1,
            device_id=(ia, wrap(ja + lax.rem(t, nja), nja), wrap(ka + t // nja, nka)),
            device_id_type=pl.DeviceIdType.MESH,
        )

    @pl.loop(nja, nia * nja)
    def _(t):
        pl.semaphore_signal(
            barrier,
            inc=1,
            device_id=(wrap(ia + t // nja, nia), wrap(ja + lax.rem(t, nja), nja), ka),
            device_id_type=pl.DeviceIdType.MESH,
        )

    col_t[...] = transposed(column_ref[...]).astype(BF16)
    pl.semaphore_wait(barrier, slots - 1 + (nia - 1) * nja)

    def pair_copy(s):
        return remote(
            coup.at[s, other], pair_in.at[s], pair_send.at[s], pair_recv.at[s], ia, ja + 1 - 2 * core, ka
        )

    def coupled_block(s):
        mat_copy(s).wait()
        block = dot_nt(col_t[...], mats[s]).reshape(groups, 2, q1, ti)
        coup[s, 0] = block[:, 0]
        coup[s, 1] = block[:, 1]
        pair_copy(s).start()

    def paired_sum(s):
        pair_copy(s).wait_recv()
        coup[s, core] = coup[s, core] + pair_in[s]

    def ring_copy(s):
        return remote(
            coup.at[s, core], ring_in.at[s], send_sem.at[0], recv_sem.at[0], block_of(s), ja, ka
        )

    coupled_block(0)

    @pl.loop(1, nia)
    def _(s):
        coupled_block(s)
        paired_sum(s - 1)
        ring_copy(s - 1).start()

    gc_loc[...] = dot(col_t[...], column_ref[...]).reshape(slots, q1, rank)
    time_tr = transposed(time_ref[...])
    time_t[...] = time_tr.reshape(nia * nja, q3, tk)
    gt_loc[...] = dot(time_tr.astype(BF16), time_ref[...]).reshape(nka, q2, rank)
    second_tr = transposed(second_ref[...])
    second_t[...] = second_tr.reshape(nka, q2, tj)
    gs_loc[...] = dot(second_tr.astype(BF16), second_ref[...]).reshape(slots, q1, rank)
    first_t[...] = transposed(first_ref[...]).reshape(slots, q1, ti)
    second_f[...] = second_ref[...].astype(F32)
    time_f[...] = time_ref[...].astype(F32)
    gc_in[slot1] = gc_loc[slot1]
    gs_in[ja] = gs_loc[slot1]
    gt_in[ka] = gt_loc[ka]

    @pl.loop(1, slots)
    def _(t):
        dja, dka = wrap(ja + lax.rem(t, nja), nja), wrap(ka + t // nja, nka)
        remote(
            gc_loc.at[dka * nja + dja], gc_in.at[slot1], send_sem.at[1], recv_sem.at[1], ia, dja, dka
        ).start()

    @pl.loop(1, nja)
    def _(t):
        dja = wrap(ja + t, nja)
        remote(
            gs_loc.at[ka * nja + dja], gs_in.at[ja], send_sem.at[2], recv_sem.at[2], ia, dja, ka
        ).start()

    @pl.loop(1, nka)
    def _(t):
        dka = wrap(ka + t, nka)
        remote(gt_loc.at[dka], gt_in.at[ka], send_sem.at[3], recv_sem.at[3], ia, ja, dka).start()

    paired_sum(nia - 1)

    rows = lax.broadcasted_iota(jnp.int32, (256, 256), 0)
    columns = lax.broadcasted_iota(jnp.int32, (256, 256), 1)
    order = (lax.rem(rows, 16) == columns // 16) & (rows // 16 == lax.rem(columns, 16))
    order = order.astype(F32).astype(BF16)

    @pl.loop(0, ti // 16)
    def _(b):
        tens_copy(b).wait()
        i0 = pl.multiple_of(b * 16, 16)
        for c in range(half // 16):
            low = tens[pl.ds(i0, 16), 16 * c : 16 * c + 16, :].reshape(256, tk)
            high = tens[pl.ds(i0, 16), half + 16 * c : half + 16 * c + 16, :].reshape(256, tk)
            block = dot(order, jnp.concatenate([low, high], axis=1))
            perm[16 * c : 16 * c + 16, pl.ds(i0, 16), :] = block.astype(BF16).reshape(16, 16, 2 * tk)

    slab_acc[...] = jnp.zeros_like(slab_acc)

    @pl.loop(0, half // 4)
    def _(b):
        total = slab_acc[...]
        for u in range(4):
            j = b * 4 + u
            khatri = jnp.concatenate(
                [time_f[...] * second_f[pl.ds(j, 1), :], time_f[...] * second_f[pl.ds(j + half, 1), :]],
                axis=0,
            ).astype(BF16)
            total = total + dot(perm[j], khatri)
        slab_acc[...] = total

    slab_tr = slab_acc[...].T.reshape(groups, 2, q1, ti)
    slab_half[0] = slab_tr[:, 0]
    slab_half[1] = slab_tr[:, 1]
    slab_copy = remote(
        slab_half.at[other], slab_in, send_sem.at[4], recv_sem.at[4], ia, ja + 1 - 2 * core, ka
    )
    slab_copy.start()

    wait_bytes(gc_in.at[pl.ds(0, slots - 1)], recv_sem.at[1])
    ga_in[ia] = jnp.sum(gc_in[...], axis=0)

    @pl.loop(1, nia)
    def _(t):
        remote(
            ga_in.at[ia], ga_in.at[ia], send_sem.at[5], recv_sem.at[5], wrap(ia + t, nia), ja, ka
        ).start()

    wait_bytes(gs_in.at[pl.ds(0, nja - 1)], recv_sem.at[2])
    wait_bytes(gt_in.at[pl.ds(0, nka - 1)], recv_sem.at[3])
    gt_sum[...] = jnp.sum(gt_in[...], axis=0).reshape(nja, q1, rank)
    gram_part = jnp.sum(gs_in[...], axis=0) * gt_sum[ja]

    wait_bytes(ring_in, recv_sem.at[0])
    slab_copy.wait_recv()
    sum_half[...] = (
        coup[nia - 1, core] + jnp.sum(ring_in[...], axis=0) + (slab_half[core] + slab_in[...])
    )
    sum_in[group] = sum_half[group]

    @pl.loop(1, groups)
    def _(t):
        dyh, dka = wrap(yh + lax.rem(t, nyh), nyh), wrap(ka + t // nyh, nka)
        remote(
            sum_half.at[dka * nyh + dyh],
            sum_in.at[group],
            send_sem.at[6],
            recv_sem.at[6],
            ia,
            2 * dyh + core,
            dka,
        ).start()

    wait_bytes(ga_in.at[pl.ds(0, nia - 1)], recv_sem.at[5])
    gram_total = gram_part + jnp.sum(ga_in[...], axis=0)
    denominator = exact_product(gram_total, first_ref[...])
    wait_bytes(sum_in.at[pl.ds(0, groups - 1)], recv_sem.at[6])
    numerator = jnp.sum(sum_in[...], axis=0)
    fn_in[slot1] = (first_t[slot1] * numerator / denominator).astype(BF16)

    @pl.loop(1, slots)
    def _(t):
        dja, dka = wrap(ja + lax.rem(t, nja), nja), wrap(ka + t // nja, nka)
        remote(
            fn_in.at[slot1], fn_in.at[slot1], send_sem.at[7], recv_sem.at[7], ia, dja, dka
        ).start()

    wait_bytes(fn_in.at[pl.ds(0, slots - 1)], recv_sem.at[7])
    fn_t = fn_in[...].astype(F32).reshape(rank, ti).astype(BF16)
    fn_rows[...] = transposed(fn_t)
    fn = fn_rows[...].astype(BF16)
    first_out[...] = fn
    gf_loc[...] = dot(fn_t, fn).reshape(nia * nja, q3, rank)
    ratio = q2 // q3
    mine = pl.ds(ka * ratio, ratio)
    gfa_in[ia] = gf_loc[mine]
    gfb_in[ia] = gf_loc[slot3]

    @pl.loop(1, nia)
    def _(t):
        dia = wrap(ia + t, nia)
        remote(gf_loc.at[mine], gfa_in.at[ia], send_sem.at[8], recv_sem.at[8], dia, ja, ka).start()
        remote(
            gf_loc.at[dia * nja + ja], gfb_in.at[ia], send_sem.at[9], recv_sem.at[9], dia, ja, ka
        ).start()

    plane[...] = jnp.zeros_like(plane)

    @pl.loop(0, ti // 8)
    def _(b):
        i0 = pl.multiple_of(b * 8, 8)
        block = dot(tens[pl.ds(i0, 8)].reshape(8 * tj, tk), time_ref[...]).reshape(8, tj, rank)
        scaled = fn_rows[pl.ds(i0, 8), :]
        total = plane[...]
        for u in range(8):
            total = total + block[u] * scaled[u : u + 1, :]
        plane[...] = total

    ps_loc[...] = plane[...].T.reshape(nka, q2, tj)
    ps_in[ka] = ps_loc[ka]

    @pl.loop(1, nka)
    def _(t):
        dka = wrap(ka + t, nka)
        remote(ps_loc.at[dka], ps_in.at[ka], send_sem.at[10], recv_sem.at[10], ia, ja, dka).start()

    def weigh(start, stop):
        @pl.loop(start, stop)
        def _(j):
            wide[j] = dot(fn_in[...].astype(F32).reshape(rank, ti).astype(BF16), perm[j])

    weigh(0, half // 2)
    wait_bytes(ps_in.at[pl.ds(0, nka - 1)], recv_sem.at[10])
    pa_in[ia] = jnp.sum(ps_in[...], axis=0)

    @pl.loop(1, nia)
    def _(t):
        remote(
            pa_in.at[ia], pa_in.at[ia], send_sem.at[11], recv_sem.at[11], wrap(ia + t, nia), ja, ka
        ).start()

    wait_bytes(gfa_in.at[pl.ds(0, nia - 1)], recv_sem.at[8])
    gram_rows = jnp.sum(gfa_in[...], axis=0).reshape(q2, rank) * gt_sum[...].reshape(q2, rank)
    second_den = exact_product(gram_rows, second_ref[...])
    weigh(half // 2, half)
    wait_bytes(pa_in.at[pl.ds(0, nia - 1)], recv_sem.at[11])
    second_num = jnp.sum(pa_in[...], axis=0)
    sn_in[ka] = (second_t[ka] * second_num / second_den).astype(BF16)

    @pl.loop(1, nka)
    def _(t):
        remote(
            sn_in.at[ka], sn_in.at[ka], send_sem.at[12], recv_sem.at[12], ia, ja, wrap(ka + t, nka)
        ).start()

    wait_bytes(sn_in.at[pl.ds(0, nka - 1)], recv_sem.at[12])
    sn_t = sn_in[...].reshape(rank, tj)
    sn_groups[...] = sn_t.reshape(nia, nja * q3, tj)
    gn_loc[...] = dot_nt(sn_groups[ia], sn_t).reshape(nja, q3, rank)
    gn_in[ja] = gn_loc[ja]

    @pl.loop(1, nja)
    def _(t):
        dja = wrap(ja + t, nja)
        remote(gn_loc.at[dja], gn_in.at[ja], send_sem.at[13], recv_sem.at[13], ia, dja, ka).start()

    tsum[...] = jnp.zeros_like(tsum)
    lane = lax.broadcasted_iota(jnp.int32, (tj, 2 * tk), 1) // tk
    row = lax.broadcasted_iota(jnp.int32, (tj, 2 * tk), 0)
    place = row - lane * half

    @pl.loop(0, half // 4)
    def _(b):
        total = tsum[...]
        for u in range(4):
            j = b * 4 + u
            pick = (place == j).astype(F32).astype(BF16)
            total = total + dot(sn_t, pick) * wide[j]
        tsum[...] = total

    ts_loc[...] = (tsum[:, :tk] + tsum[:, tk:]).reshape(nia * nja, q3, tk)
    ts_in[slot3] = ts_loc[slot3]

    @pl.loop(1, nia * nja)
    def _(t):
        dia, dja = wrap(ia + t // nja, nia), wrap(ja + lax.rem(t, nja), nja)
        remote(
            ts_loc.at[dia * nja + dja], ts_in.at[slot3], send_sem.at[14], recv_sem.at[14], dia, dja, ka
        ).start()

    second_out[...] = transposed(sn_t).astype(BF16)
    wait_bytes(gfb_in.at[pl.ds(0, nia - 1)], recv_sem.at[9])
    wait_bytes(gn_in.at[pl.ds(0, nja - 1)], recv_sem.at[13])
    gram_rows = jnp.sum(gfb_in[...], axis=0) * jnp.sum(gn_in[...], axis=0)
    time_den = exact_product(gram_rows, time_ref[...])
    wait_bytes(ts_in.at[pl.ds(0, nia * nja - 1)], recv_sem.at[14])
    time_num = jnp.sum(ts_in[...], axis=0)
    tn_in[slot3] = (time_t[slot3] * time_num / time_den).astype(BF16)

    @pl.loop(1, nia * nja)
    def _(t):
        dia, dja = wrap(ia + t // nja, nia), wrap(ja + lax.rem(t, nja), nja)
        remote(
            tn_in.at[slot3], tn_in.at[slot3], send_sem.at[15], recv_sem.at[15], dia, dja, ka
        ).start()

    @pl.loop(0, nia)
    def _(s):
        pair_copy(s).wait_send()

    slab_copy.wait_send()
    for place_, ref in (
        (0, ring_in),
        (1, gc_in.at[pl.ds(0, slots - 1)]),
        (2, gs_in.at[pl.ds(0, nja - 1)]),
        (3, gt_in.at[pl.ds(0, nka - 1)]),
        (5, ga_in.at[pl.ds(0, nia - 1)]),
        (6, sum_in.at[pl.ds(0, groups - 1)]),
        (7, fn_in.at[pl.ds(0, slots - 1)]),
        (8, gfa_in.at[pl.ds(0, nia - 1)]),
        (9, gfb_in.at[pl.ds(0, nia - 1)]),
        (10, ps_in.at[pl.ds(0, nka - 1)]),
        (11, pa_in.at[pl.ds(0, nia - 1)]),
        (12, sn_in.at[pl.ds(0, nka - 1)]),
        (13, gn_in.at[pl.ds(0, nja - 1)]),
        (14, ts_in.at[pl.ds(0, nia * nja - 1)]),
        (15, tn_in.at[pl.ds(0, nia * nja - 1)]),
    ):
        wait_bytes(ref, send_sem.at[place_])

    wait_bytes(tn_in.at[pl.ds(0, nia * nja - 1)], recv_sem.at[15])
    tn_t = tn_in[...].astype(F32).reshape(rank, tk).astype(BF16)
    time_out[...] = transposed(tn_t).astype(BF16)


def on_device(nia, nja, nka, tensor, matrix, first_factor, second_factor, time_factor, column_factor):
    ti, tj, tk = tensor.shape
    rank = first_factor.shape[1]
    depth = column_factor.shape[0]
    nyh = nja // 2
    slots = nja * nka
    q1, q2, q3 = rank // slots, rank // nka, rank // (nia * nja)
    groups = nka * nyh
    half = tj // 2
    V = pltpu.VMEM
    scratch = [
        V((ti, tj, tk), BF16),
        V((half, ti, 2 * tk), BF16),
        V((half, rank, 2 * tk), F32),
        V((nia, ti, depth), BF16),
        V((rank, depth), BF16),
        V((nia, 2, groups, q1, ti), F32),
        V((nia, groups, q1, ti), F32),
        V((nia - 1, groups, q1, ti), F32),
        V((ti, rank), F32),
        V((2, groups, q1, ti), F32),
        V((groups, q1, ti), F32),
        V((groups, q1, ti), F32),
        V((groups, q1, ti), F32),
        V((slots, q1, rank), F32),
        V((slots, q1, rank), F32),
        V((slots, q1, rank), F32),
        V((nja, q1, rank), F32),
        V((nka, q2, rank), F32),
        V((nka, q2, rank), F32),
        V((nja, q1, rank), F32),
        V((nia, q1, rank), F32),
        V((slots, q1, ti), F32),
        V((nka, q2, tj), F32),
        V((nia * nja, q3, tk), F32),
        V((tj, rank), F32),
        V((tk, rank), F32),
        V((slots, q1, ti), BF16),
        V((ti, rank), F32),
        V((nia * nja, q3, rank), F32),
        V((nia, q2 // q3, q3, rank), F32),
        V((nia, q3, rank), F32),
        V((tj, rank), F32),
        V((nka, q2, tj), F32),
        V((nka, q2, tj), F32),
        V((nia, q2, tj), F32),
        V((nka, q2, tj), BF16),
        V((nia, nja * q3, tj), BF16),
        V((nja, q3, rank), F32),
        V((nja, q3, rank), F32),
        V((rank, 2 * tk), F32),
        V((nia * nja, q3, tk), F32),
        V((nia * nja, q3, tk), F32),
        V((nia * nja, q3, tk), BF16),
        pltpu.SemaphoreType.DMA((nia,)),
        pltpu.SemaphoreType.DMA((ti // 16,)),
        pltpu.SemaphoreType.DMA((nia,)),
        pltpu.SemaphoreType.DMA((nia,)),
        pltpu.SemaphoreType.DMA((16,)),
        pltpu.SemaphoreType.DMA((16,)),
    ]
    in_vmem = pl.BlockSpec(memory_space=pltpu.VMEM)
    in_place = pl.BlockSpec(memory_space=pl.ANY)
    return pl.pallas_call(
        functools.partial(kernel, (nia, nja, nka, rank, ti, tj, tk)),
        out_shape=(
            jax.ShapeDtypeStruct((ti, rank), BF16),
            jax.ShapeDtypeStruct((tj, rank), BF16),
            jax.ShapeDtypeStruct((tk, rank), BF16),
        ),
        in_specs=[in_place, in_place, in_vmem, in_vmem, in_vmem, in_vmem],
        out_specs=(in_vmem, in_vmem, in_vmem),
        scratch_shapes=scratch,
        compiler_params=pltpu.CompilerParams(
            collective_id=0, has_side_effects=True, vmem_limit_bytes=60 * 1024 * 1024
        ),
        name="factor_round",
    )(tensor, matrix, first_factor, second_factor, time_factor, column_factor)


def solution(mesh):
    sizes = (mesh.shape["ia"], mesh.shape["ja"], mesh.shape["ka"])
    return jax.shard_map(
        functools.partial(on_device, *sizes),
        mesh=mesh,
        in_specs=(
            P("ia", "ja", "ka"),
            P(None, ("ia", "ja", "ka")),
            P("ia", None),
            P("ja", None),
            P("ka", None),
            P(("ia", "ja", "ka"), None),
        ),
        out_specs=(P("ia", None), P("ja", None), P("ka", None)),
        check_vma=False,
    )
```

```python
import functools

import jax
import jax.numpy as jnp
from jax import lax
from jax.experimental import pallas as pl
from jax.experimental.pallas import tpu as pltpu
from jax.sharding import PartitionSpec as P

F32 = jnp.float32
BF16 = jnp.bfloat16


def dot(a, b):
    return jnp.dot(a, b, preferred_element_type=F32)


def dot_nt(a, b):
    return lax.dot_general(a, b, (((1,), (1,)), ((), ())), preferred_element_type=F32)


def identity(n):
    rows = lax.broadcasted_iota(jnp.int32, (n, n), 0)
    columns = lax.broadcasted_iota(jnp.int32, (n, n), 1)
    return (rows == columns).astype(F32).astype(BF16)


def transposed(values):
    return dot_nt(identity(values.shape[1]), values)


def exact_product(gram, factor):
    rows = gram.shape[0]
    high = gram.astype(BF16).astype(F32)
    rest = gram - high
    middle = rest.astype(BF16).astype(F32)
    low = (rest - middle).astype(BF16).astype(F32)
    parts = [high, middle, low]
    while (rows * len(parts)) % 16:
        parts.append(jnp.zeros_like(high))
    stacked = dot_nt(jnp.concatenate(parts, axis=0).astype(BF16), factor)
    return stacked[:rows] + (stacked[rows : 2 * rows] + stacked[2 * rows : 3 * rows])


def kernel(
    sizes,
    tensor_ref,
    matrix_ref,
    first_ref,
    second_ref,
    time_ref,
    column_ref,
    first_out,
    second_out,
    time_out,
    tens,
    perm,
    turn,
    wide,
    mats,
    col_t,
    coup,
    pair_in,
    ring_in,
    slab_acc,
    slab_half,
    slab_in,
    sum_half,
    sum_in,
    gc_loc,
    gc_in,
    gs_loc,
    gs_in,
    gt_loc,
    gt_in,
    gt_sum,
    ga_in,
    first_t,
    second_t,
    time_t,
    second_f,
    time_f,
    fn_in,
    gf_loc,
    gfa_in,
    gfb_in,
    plane,
    ps_loc,
    ps_in,
    pa_in,
    sn_in,
    sn_groups,
    gn_loc,
    gn_in,
    sn_f,
    ts_loc,
    ts_in,
    tn_in,
    mat_sem,
    tens_sem,
    pair_send,
    pair_recv,
    send_sem,
    recv_sem,
):
    nia, nja, nka, rank, ti, tj, tk = sizes
    nyh = nja // 2
    slots = nja * nka
    q1, q2, q3 = rank // slots, rank // nka, rank // (nia * nja)
    groups = nka * nyh
    half = tj // 2
    ia, ja, ka = lax.axis_index("ia"), lax.axis_index("ja"), lax.axis_index("ka")
    core = lax.rem(ja, 2)
    other = 1 - core
    yh = ja // 2
    slot1 = ka * nja + ja
    group = ka * nyh + yh
    slot3 = ia * nja + ja

    def wrap(value, n):
        return lax.rem(value + n, n)

    def remote(src, dst, s_sem, r_sem, dia, dja, dka):
        return pltpu.make_async_remote_copy(
            src_ref=src,
            dst_ref=dst,
            send_sem=s_sem,
            recv_sem=r_sem,
            device_id=(dia, dja, dka),
            device_id_type=pl.DeviceIdType.MESH,
        )

    def wait_bytes(ref, sem):
        pltpu.make_async_copy(ref, ref, sem).wait()

    def block_of(s):
        return wrap(ia + 1 + s, nia)

    def mat_copy(s):
        rows = pl.ds(pl.multiple_of(block_of(s) * ti, ti), ti)
        return pltpu.make_async_copy(matrix_ref.at[rows, :], mats.at[s], mat_sem.at[s])

    def tens_copy(b):
        rows = pl.ds(b * 16, 16)
        return pltpu.make_async_copy(tensor_ref.at[rows], tens.at[rows], tens_sem.at[b])

    @pl.loop(0, nia)
    def _(s):
        mat_copy(s).start()

    @pl.loop(0, ti // 16)
    def _(b):
        tens_copy(b).start()

    barrier = pltpu.get_barrier_semaphore()

    @pl.loop(1, slots)
    def _(t):
        pl.semaphore_signal(
            barrier,
            inc=1,
            device_id=(ia, wrap(ja + lax.rem(t, nja), nja), wrap(ka + t // nja, nka)),
            device_id_type=pl.DeviceIdType.MESH,
        )

    @pl.loop(nja, nia * nja)
    def _(t):
        pl.semaphore_signal(
            barrier,
            inc=1,
            device_id=(wrap(ia + t // nja, nia), wrap(ja + lax.rem(t, nja), nja), ka),
            device_id_type=pl.DeviceIdType.MESH,
        )

    col_t[...] = transposed(column_ref[...]).astype(BF16)

    def pair_copy(s):
        return remote(
            coup.at[s, other], pair_in.at[s], pair_send.at[s], pair_recv.at[s], ia, ja + 1 - 2 * core, ka
        )

    def coupled_block(s):
        mat_copy(s).wait()
        block = dot_nt(col_t[...], mats[s]).reshape(groups, 2, q1, ti)
        coup[s, 0] = block[:, 0]
        coup[s, 1] = block[:, 1]

    def paired_sum(s):
        pair_copy(s).wait_recv()
        coup[s, core] = coup[s, core] + pair_in[s]

    def ring_copy(s):
        return remote(
            coup.at[s, core], ring_in.at[s], send_sem.at[0], recv_sem.at[0], block_of(s), ja, ka
        )

    @pl.loop(0, nia)
    def _(s):
        coupled_block(s)

    gc_loc[...] = dot(col_t[...], column_ref[...]).reshape(slots, q1, rank)
    time_tr = transposed(time_ref[...])
    time_t[...] = time_tr.reshape(nia * nja, q3, tk)
    gt_loc[...] = dot(time_tr.astype(BF16), time_ref[...]).reshape(nka, q2, rank)
    second_tr = transposed(second_ref[...])
    second_t[...] = second_tr.reshape(nka, q2, tj)
    gs_loc[...] = dot(second_tr.astype(BF16), second_ref[...]).reshape(slots, q1, rank)
    first_t[...] = transposed(first_ref[...]).reshape(slots, q1, ti)
    second_f[...] = second_ref[...].astype(F32)
    time_f[...] = time_ref[...].astype(F32)
    gc_in[slot1] = gc_loc[slot1]
    gs_in[ja] = gs_loc[slot1]
    gt_in[ka] = gt_loc[ka]
    pl.semaphore_wait(barrier, slots - 1 + (nia - 1) * nja)

    @pl.loop(0, nia)
    def _(s):
        pair_copy(s).start()

    @pl.loop(0, nia - 1)
    def _(s):
        paired_sum(s)
        ring_copy(s).start()

    @pl.loop(1, slots)
    def _(t):
        dja, dka = wrap(ja + lax.rem(t, nja), nja), wrap(ka + t // nja, nka)
        remote(
            gc_loc.at[dka * nja + dja], gc_in.at[slot1], send_sem.at[1], recv_sem.at[1], ia, dja, dka
        ).start()

    @pl.loop(1, nja)
    def _(t):
        dja = wrap(ja + t, nja)
        remote(
            gs_loc.at[ka * nja + dja], gs_in.at[ja], send_sem.at[2], recv_sem.at[2], ia, dja, ka
        ).start()

    @pl.loop(1, nka)
    def _(t):
        dka = wrap(ka + t, nka)
        remote(gt_loc.at[dka], gt_in.at[ka], send_sem.at[3], recv_sem.at[3], ia, ja, dka).start()

    paired_sum(nia - 1)

    rows = lax.broadcasted_iota(jnp.int32, (256, 256), 0)
    columns = lax.broadcasted_iota(jnp.int32, (256, 256), 1)
    order = (lax.rem(rows, 16) == columns // 16) & (rows // 16 == lax.rem(columns, 16))
    order = order.astype(F32).astype(BF16)

    @pl.loop(0, ti // 16)
    def _(b):
        tens_copy(b).wait()
        i0 = pl.multiple_of(b * 16, 16)
        for c in range(half // 16):
            low = tens[pl.ds(i0, 16), 16 * c : 16 * c + 16, :].reshape(256, tk)
            high = tens[pl.ds(i0, 16), half + 16 * c : half + 16 * c + 16, :].reshape(256, tk)
            block = dot(order, jnp.concatenate([low, high], axis=1))
            perm[16 * c : 16 * c + 16, pl.ds(i0, 16), :] = block.astype(BF16).reshape(16, 16, 2 * tk)

    slab_acc[...] = jnp.zeros_like(slab_acc)

    @pl.loop(0, half // 4)
    def _(b):
        total = slab_acc[...]
        for u in range(4):
            j = b * 4 + u
            khatri = jnp.concatenate(
                [time_f[...] * second_f[pl.ds(j, 1), :], time_f[...] * second_f[pl.ds(j + half, 1), :]],
                axis=0,
            ).astype(BF16)
            total = total + dot(perm[j], khatri)
        slab_acc[...] = total

    slab_tr = slab_acc[...].T.reshape(groups, 2, q1, ti)
    slab_half[0] = slab_tr[:, 0]
    slab_half[1] = slab_tr[:, 1]
    slab_copy = remote(
        slab_half.at[other], slab_in, send_sem.at[4], recv_sem.at[4], ia, ja + 1 - 2 * core, ka
    )
    slab_copy.start()

    unit = identity(2 * tk)

    def turn_blocks(start, stop):
        @pl.loop(start, stop)
        def _(b):
            for u in range(4):
                turn[4 * b + u] = dot_nt(unit, perm[4 * b + u]).astype(BF16)

    wait_bytes(gc_in.at[pl.ds(0, slots - 1)], recv_sem.at[1])
    ga_in[ia] = jnp.sum(gc_in[...], axis=0)

    @pl.loop(1, nia)
    def _(t):
        remote(
            ga_in.at[ia], ga_in.at[ia], send_sem.at[5], recv_sem.at[5], wrap(ia + t, nia), ja, ka
        ).start()

    wait_bytes(gs_in.at[pl.ds(0, nja - 1)], recv_sem.at[2])
    wait_bytes(gt_in.at[pl.ds(0, nka - 1)], recv_sem.at[3])
    gt_sum[...] = jnp.sum(gt_in[...], axis=0).reshape(nja, q1, rank)
    gram_part = jnp.sum(gs_in[...], axis=0) * gt_sum[ja]

    wait_bytes(ring_in, recv_sem.at[0])
    slab_copy.wait_recv()
    sum_half[...] = (
        coup[nia - 1, core] + jnp.sum(ring_in[...], axis=0) + (slab_half[core] + slab_in[...])
    )
    sum_in[group] = sum_half[group]

    @pl.loop(1, groups)
    def _(t):
        dyh, dka = wrap(yh + lax.rem(t, nyh), nyh), wrap(ka + t // nyh, nka)
        remote(
            sum_half.at[dka * nyh + dyh],
            sum_in.at[group],
            send_sem.at[6],
            recv_sem.at[6],
            ia,
            2 * dyh + core,
            dka,
        ).start()

    turn_blocks(0, half // 8)
    wait_bytes(ga_in.at[pl.ds(0, nia - 1)], recv_sem.at[5])
    gram_total = gram_part + jnp.sum(ga_in[...], axis=0)
    denominator = exact_product(gram_total, first_ref[...])
    wait_bytes(sum_in.at[pl.ds(0, groups - 1)], recv_sem.at[6])
    numerator = jnp.sum(sum_in[...], axis=0)
    fn_in[slot1] = (first_t[slot1] * numerator / denominator).astype(BF16)

    @pl.loop(1, slots)
    def _(t):
        dja, dka = wrap(ja + lax.rem(t, nja), nja), wrap(ka + t // nja, nka)
        remote(
            fn_in.at[slot1], fn_in.at[slot1], send_sem.at[7], recv_sem.at[7], ia, dja, dka
        ).start()

    turn_blocks(half // 8, half // 4)
    wait_bytes(fn_in.at[pl.ds(0, slots - 1)], recv_sem.at[7])
    fn_t = fn_in[...].astype(F32).reshape(rank, ti).astype(BF16)
    fn = transposed(fn_t).astype(BF16)
    first_out[...] = fn
    gf_loc[...] = dot(fn_t, fn).reshape(nia * nja, q3, rank)
    ratio = q2 // q3
    mine = pl.ds(ka * ratio, ratio)
    gfa_in[ia] = gf_loc[mine]
    gfb_in[ia] = gf_loc[slot3]

    @pl.loop(1, nia)
    def _(t):
        dia = wrap(ia + t, nia)
        remote(gf_loc.at[mine], gfa_in.at[ia], send_sem.at[8], recv_sem.at[8], dia, ja, ka).start()
        remote(
            gf_loc.at[dia * nja + ja], gfb_in.at[ia], send_sem.at[9], recv_sem.at[9], dia, ja, ka
        ).start()

    @pl.loop(0, half // 4)
    def _(b):
        for u in range(4):
            j = b * 4 + u
            block = dot(turn[j], first_out[...])
            wide[j] = block
            sums = jnp.sum(block.reshape(2, tk, rank) * time_f[...][None], axis=1)
            plane[pl.ds(j, 1), :] = sums[0:1]
            plane[pl.ds(j + half, 1), :] = sums[1:2]

    ps_loc[...] = plane[...].T.reshape(nka, q2, tj)
    ps_in[ka] = ps_loc[ka]

    @pl.loop(1, nka)
    def _(t):
        dka = wrap(ka + t, nka)
        remote(ps_loc.at[dka], ps_in.at[ka], send_sem.at[10], recv_sem.at[10], ia, ja, dka).start()

    wait_bytes(ps_in.at[pl.ds(0, nka - 1)], recv_sem.at[10])
    pa_in[ia] = jnp.sum(ps_in[...], axis=0)

    @pl.loop(1, nia)
    def _(t):
        remote(
            pa_in.at[ia], pa_in.at[ia], send_sem.at[11], recv_sem.at[11], wrap(ia + t, nia), ja, ka
        ).start()

    wait_bytes(gfa_in.at[pl.ds(0, nia - 1)], recv_sem.at[8])
    gram_rows = jnp.sum(gfa_in[...], axis=0).reshape(q2, rank) * gt_sum[...].reshape(q2, rank)
    second_den = exact_product(gram_rows, second_ref[...])
    wait_bytes(pa_in.at[pl.ds(0, nia - 1)], recv_sem.at[11])
    second_num = jnp.sum(pa_in[...], axis=0)
    sn_in[ka] = (second_t[ka] * second_num / second_den).astype(BF16)

    @pl.loop(1, nka)
    def _(t):
        remote(
            sn_in.at[ka], sn_in.at[ka], send_sem.at[12], recv_sem.at[12], ia, ja, wrap(ka + t, nka)
        ).start()

    wait_bytes(sn_in.at[pl.ds(0, nka - 1)], recv_sem.at[12])
    sn_t = sn_in[...].reshape(rank, tj)
    sn_groups[...] = sn_t.reshape(nia, nja * q3, tj)
    gn_loc[...] = dot_nt(sn_groups[ia], sn_t).reshape(nja, q3, rank)
    gn_in[ja] = gn_loc[ja]

    @pl.loop(1, nja)
    def _(t):
        dja = wrap(ja + t, nja)
        remote(gn_loc.at[dja], gn_in.at[ja], send_sem.at[13], recv_sem.at[13], ia, dja, ka).start()

    sn_rows = transposed(sn_t)
    second_out[...] = sn_rows.astype(BF16)
    sn_f[...] = sn_rows

    def add_planes(b, total):
        for u in range(4):
            j = b * 4 + u
            total = total + wide[j, :tk] * sn_f[pl.ds(j, 1), :]
            total = total + wide[j, tk:] * sn_f[pl.ds(j + half, 1), :]
        return total

    tsum = lax.fori_loop(0, half // 4, add_planes, jnp.zeros((tk, rank), F32))
    ts_loc[...] = tsum.T.reshape(nia * nja, q3, tk)
    ts_in[slot3] = ts_loc[slot3]

    @pl.loop(1, nia * nja)
    def _(t):
        dia, dja = wrap(ia + t // nja, nia), wrap(ja + lax.rem(t, nja), nja)
        remote(
            ts_loc.at[dia * nja + dja], ts_in.at[slot3], send_sem.at[14], recv_sem.at[14], dia, dja, ka
        ).start()

    wait_bytes(gfb_in.at[pl.ds(0, nia - 1)], recv_sem.at[9])
    wait_bytes(gn_in.at[pl.ds(0, nja - 1)], recv_sem.at[13])
    gram_rows = jnp.sum(gfb_in[...], axis=0) * jnp.sum(gn_in[...], axis=0)
    time_den = exact_product(gram_rows, time_ref[...])
    wait_bytes(ts_in.at[pl.ds(0, nia * nja - 1)], recv_sem.at[14])
    time_num = jnp.sum(ts_in[...], axis=0)
    tn_in[slot3] = (time_t[slot3] * time_num / time_den).astype(BF16)

    @pl.loop(1, nia * nja)
    def _(t):
        dia, dja = wrap(ia + t // nja, nia), wrap(ja + lax.rem(t, nja), nja)
        remote(
            tn_in.at[slot3], tn_in.at[slot3], send_sem.at[15], recv_sem.at[15], dia, dja, ka
        ).start()

    @pl.loop(0, nia)
    def _(s):
        pair_copy(s).wait_send()

    slab_copy.wait_send()
    for place_, ref in (
        (0, ring_in),
        (1, gc_in.at[pl.ds(0, slots - 1)]),
        (2, gs_in.at[pl.ds(0, nja - 1)]),
        (3, gt_in.at[pl.ds(0, nka - 1)]),
        (5, ga_in.at[pl.ds(0, nia - 1)]),
        (6, sum_in.at[pl.ds(0, groups - 1)]),
        (7, fn_in.at[pl.ds(0, slots - 1)]),
        (8, gfa_in.at[pl.ds(0, nia - 1)]),
        (9, gfb_in.at[pl.ds(0, nia - 1)]),
        (10, ps_in.at[pl.ds(0, nka - 1)]),
        (11, pa_in.at[pl.ds(0, nia - 1)]),
        (12, sn_in.at[pl.ds(0, nka - 1)]),
        (13, gn_in.at[pl.ds(0, nja - 1)]),
        (14, ts_in.at[pl.ds(0, nia * nja - 1)]),
        (15, tn_in.at[pl.ds(0, nia * nja - 1)]),
    ):
        wait_bytes(ref, send_sem.at[place_])

    wait_bytes(tn_in.at[pl.ds(0, nia * nja - 1)], recv_sem.at[15])
    tn_t = tn_in[...].astype(F32).reshape(rank, tk).astype(BF16)
    time_out[...] = transposed(tn_t).astype(BF16)


def hand_out(first, second, time, first_out, second_out, time_out, sem):
    pairs = ((first, first_out), (second, second_out), (time, time_out))
    copies = [pltpu.make_async_copy(a, b, sem.at[n]) for n, (a, b) in enumerate(pairs)]
    for copy in copies:
        copy.start()
    for copy in copies:
        copy.wait()


def on_device(nia, nja, nka, tensor, matrix, first_factor, second_factor, time_factor, column_factor):
    ti, tj, tk = tensor.shape
    rank = first_factor.shape[1]
    depth = column_factor.shape[0]
    nyh = nja // 2
    slots = nja * nka
    q1, q2, q3 = rank // slots, rank // nka, rank // (nia * nja)
    groups = nka * nyh
    half = tj // 2
    V = pltpu.VMEM
    scratch = [
        V((ti, tj, tk), BF16),
        V((half, ti, 2 * tk), BF16),
        V((half, 2 * tk, ti), BF16),
        V((half, 2 * tk, rank), F32),
        V((nia, ti, depth), BF16),
        V((rank, depth), BF16),
        V((nia, 2, groups, q1, ti), F32),
        V((nia, groups, q1, ti), F32),
        V((nia - 1, groups, q1, ti), F32),
        V((ti, rank), F32),
        V((2, groups, q1, ti), F32),
        V((groups, q1, ti), F32),
        V((groups, q1, ti), F32),
        V((groups, q1, ti), F32),
        V((slots, q1, rank), F32),
        V((slots, q1, rank), F32),
        V((slots, q1, rank), F32),
        V((nja, q1, rank), F32),
        V((nka, q2, rank), F32),
        V((nka, q2, rank), F32),
        V((nja, q1, rank), F32),
        V((nia, q1, rank), F32),
        V((slots, q1, ti), F32),
        V((nka, q2, tj), F32),
        V((nia * nja, q3, tk), F32),
        V((tj, rank), F32),
        V((tk, rank), F32),
        V((slots, q1, ti), BF16),
        V((nia * nja, q3, rank), F32),
        V((nia, q2 // q3, q3, rank), F32),
        V((nia, q3, rank), F32),
        V((tj, rank), F32),
        V((nka, q2, tj), F32),
        V((nka, q2, tj), F32),
        V((nia, q2, tj), F32),
        V((nka, q2, tj), BF16),
        V((nia, nja * q3, tj), BF16),
        V((nja, q3, rank), F32),
        V((nja, q3, rank), F32),
        V((tj, rank), F32),
        V((nia * nja, q3, tk), F32),
        V((nia * nja, q3, tk), F32),
        V((nia * nja, q3, tk), BF16),
        pltpu.SemaphoreType.DMA((nia,)),
        pltpu.SemaphoreType.DMA((ti // 16,)),
        pltpu.SemaphoreType.DMA((nia,)),
        pltpu.SemaphoreType.DMA((nia,)),
        pltpu.SemaphoreType.DMA((16,)),
        pltpu.SemaphoreType.DMA((16,)),
    ]
    in_vmem = pl.BlockSpec(memory_space=pltpu.VMEM)
    in_place = pl.BlockSpec(memory_space=pl.ANY)
    shapes = (
        jax.ShapeDtypeStruct((ti, rank), BF16),
        jax.ShapeDtypeStruct((tj, rank), BF16),
        jax.ShapeDtypeStruct((tk, rank), BF16),
    )
    results = pl.pallas_call(
        functools.partial(kernel, (nia, nja, nka, rank, ti, tj, tk)),
        out_shape=shapes,
        in_specs=[in_place, in_place, in_vmem, in_vmem, in_vmem, in_vmem],
        out_specs=(in_vmem, in_vmem, in_vmem),
        scratch_shapes=scratch,
        compiler_params=pltpu.CompilerParams(
            collective_id=0, has_side_effects=True, vmem_limit_bytes=60 * 1024 * 1024
        ),
        name="factor_round",
    )(tensor, matrix, first_factor, second_factor, time_factor, column_factor)
    return pl.pallas_call(
        hand_out,
        out_shape=shapes,
        in_specs=[in_place] * 3,
        out_specs=(in_place,) * 3,
        scratch_shapes=[pltpu.SemaphoreType.DMA((3,))],
        name="hand_out",
    )(*results)


def solution(mesh):
    sizes = (mesh.shape["ia"], mesh.shape["ja"], mesh.shape["ka"])
    return jax.shard_map(
        functools.partial(on_device, *sizes),
        mesh=mesh,
        in_specs=(
            P("ia", "ja", "ka"),
            P(None, ("ia", "ja", "ka")),
            P("ia", None),
            P("ja", None),
            P("ka", None),
            P(("ia", "ja", "ka"), None),
        ),
        out_specs=(P("ia", None), P("ja", None), P("ka", None)),
        check_vma=False,
    )
```

```python
import functools

import jax
import jax.numpy as jnp
from jax import lax
from jax.experimental import pallas as pl
from jax.experimental.pallas import tpu as pltpu
from jax.sharding import PartitionSpec as P

F32 = jnp.float32
BF16 = jnp.bfloat16


def dot(a, b):
    return jnp.dot(a, b, preferred_element_type=F32)


def dot_nt(a, b):
    return lax.dot_general(a, b, (((1,), (1,)), ((), ())), preferred_element_type=F32)


def identity(n):
    rows = lax.broadcasted_iota(jnp.int32, (n, n), 0)
    columns = lax.broadcasted_iota(jnp.int32, (n, n), 1)
    return (rows == columns).astype(F32).astype(BF16)


def transposed(values):
    return dot_nt(identity(values.shape[1]), values)


def exact_product(gram, factor):
    rows = gram.shape[0]
    high = gram.astype(BF16).astype(F32)
    rest = gram - high
    middle = rest.astype(BF16).astype(F32)
    low = (rest - middle).astype(BF16).astype(F32)
    parts = [high, middle, low]
    while (rows * len(parts)) % 16:
        parts.append(jnp.zeros_like(high))
    stacked = dot_nt(jnp.concatenate(parts, axis=0).astype(BF16), factor)
    return stacked[:rows] + (stacked[rows : 2 * rows] + stacked[2 * rows : 3 * rows])


def kernel(
    sizes,
    tensor_ref,
    matrix_ref,
    first_ref,
    second_ref,
    time_ref,
    column_ref,
    first_out,
    second_out,
    time_out,
    tens,
    perm,
    turn,
    wide,
    mats,
    col_t,
    coup,
    pair_in,
    ring_in,
    slab_acc,
    slab_half,
    slab_in,
    sum_half,
    sum_in,
    gc_loc,
    gc_pair,
    gc_half,
    gc_in,
    gs_loc,
    gs_in,
    gt_loc,
    gt_in,
    gt_wide,
    ga_in,
    first_t,
    second_t,
    time_t,
    second_f,
    time_f,
    fn_in,
    gf_loc,
    gf_in,
    gf_sum,
    plane,
    ps_loc,
    ps_in,
    pa_in,
    sn_in,
    gn_loc,
    gn_in,
    sn_f,
    ts_loc,
    ts_in,
    tn_in,
    mat_sem,
    tens_sem,
    pair_send,
    pair_recv,
    send_sem,
    recv_sem,
):
    nia, nja, nka, rank, ti, tj, tk = sizes
    nyh = nja // 2
    nx = nia // 2
    slots = nja * nka
    q1, q3 = rank // slots, rank // (nia * nja)
    q4 = nja * q3
    groups = nka * nyh
    half = tj // 2
    ia, ja, ka = lax.axis_index("ia"), lax.axis_index("ja"), lax.axis_index("ka")
    core = lax.rem(ja, 2)
    other = 1 - core
    yh = ja // 2
    slot1 = ka * nja + ja
    group = ka * nyh + yh
    slot3 = ia * nja + ja

    def wrap(value, n):
        return lax.rem(value + n, n)

    def far(u, n):
        return n // 2 + (1 - 2 * lax.rem(u, 2)) * ((u + 1) // 2)

    def ia_of(u):
        row = wrap(ia // nx + 1 - u // nx, 2)
        return row * nx + wrap(lax.rem(ia, nx) + far(lax.rem(u, nx), nx), nx)

    def ka_of(u):
        return wrap(ka + far(u, nka), nka)

    def group_of(t):
        return wrap(yh + nyh - 1 - lax.rem(t, nyh), nyh), ka_of(t // nyh)

    def plane_of(t):
        return ia_of(t // nja), wrap(ja + far(lax.rem(t, nja), nja), nja)

    def remote(src, dst, s_sem, r_sem, dia, dja, dka):
        return pltpu.make_async_remote_copy(
            src_ref=src,
            dst_ref=dst,
            send_sem=s_sem,
            recv_sem=r_sem,
            device_id=(dia, dja, dka),
            device_id_type=pl.DeviceIdType.MESH,
        )

    def wait_bytes(ref, sem):
        pltpu.make_async_copy(ref, ref, sem).wait()

    sibling = ja + 1 - 2 * core
    block_of = ia_of

    def mat_copy(s):
        rows = pl.ds(pl.multiple_of(block_of(s) * ti, ti), ti)
        return pltpu.make_async_copy(matrix_ref.at[rows, :], mats.at[s], mat_sem.at[s])

    def tens_copy(b):
        rows = pl.ds(b * 16, 16)
        return pltpu.make_async_copy(tensor_ref.at[rows], tens.at[rows], tens_sem.at[b])

    @pl.loop(0, nia)
    def _(s):
        mat_copy(s).start()

    @pl.loop(0, ti // 16)
    def _(b):
        tens_copy(b).start()

    barrier = pltpu.get_barrier_semaphore()

    def greet(dia, dja, dka):
        pl.semaphore_signal(
            barrier, inc=1, device_id=(dia, dja, dka), device_id_type=pl.DeviceIdType.MESH
        )

    @pl.loop(0, groups - 1)
    def _(t):
        dyh, dka = group_of(t)
        greet(ia, 2 * dyh + core, dka)

    @pl.loop(0, (nia - 1) * nja)
    def _(t):
        dia, dja = plane_of(t)
        greet(dia, dja, ka)

    greet(ia, 2 * (1 - yh) + other, ka)
    greet(ia, sibling, ka)
    col_t[...] = transposed(column_ref[...]).astype(BF16)

    def pair_copy(s):
        return remote(
            coup.at[s, other], pair_in.at[s], pair_send.at[s], pair_recv.at[s], ia, sibling, ka
        )

    def coupled_block(s):
        mat_copy(s).wait()
        block = dot_nt(col_t[...], mats[s]).reshape(groups, 2, q1, ti)
        coup[s, 0] = block[:, 0]
        coup[s, 1] = block[:, 1]

    def paired_sum(s):
        pair_copy(s).wait_recv()
        coup[s, core] = coup[s, core] + pair_in[s]

    def ring_copy(s):
        return remote(
            coup.at[s, core], ring_in.at[s], send_sem.at[0], recv_sem.at[0], block_of(s), ja, ka
        )

    @pl.loop(0, nia)
    def _(s):
        coupled_block(s)

    pl.semaphore_wait(barrier, groups - 1 + (nia - 1) * nja + 2)

    @pl.loop(0, nia)
    def _(s):
        pair_copy(s).start()

    gram = dot(col_t[...], column_ref[...]).reshape(groups, 2, q1, rank)
    gc_loc[0] = gram[:, 0]
    gc_loc[1] = gram[:, 1]
    gc_copy = remote(gc_loc.at[other], gc_pair, send_sem.at[9], recv_sem.at[9], ia, sibling, ka)
    gc_copy.start()

    @pl.loop(0, nia - 1)
    def _(s):
        paired_sum(s)
        ring_copy(s).start()

    time_tr = transposed(time_ref[...])
    time_t[...] = time_tr.reshape(nia * nja, q3, tk)
    gt_loc[...] = dot(time_tr.astype(BF16), time_ref[...]).reshape(slots, q1, rank)
    mine = pl.ds(ia * (q4 // q1), q4 // q1)
    gt_in[ka] = gt_loc[slot1]
    gt_wide[ka] = gt_loc[mine]

    @pl.loop(0, nka - 1)
    def _(t):
        dka = ka_of(t)
        remote(
            gt_loc.at[dka * nja + ja], gt_in.at[ka], send_sem.at[3], recv_sem.at[3], ia, ja, dka
        ).start()
        remote(gt_loc.at[mine], gt_wide.at[ka], send_sem.at[8], recv_sem.at[8], ia, ja, dka).start()

    gc_copy.wait_recv()
    gc_half[...] = gc_loc[core] + gc_pair[...]
    gc_in[group] = gc_half[group]

    @pl.loop(0, groups - 1)
    def _(t):
        dyh, dka = group_of(t)
        remote(
            gc_half.at[dka * nyh + dyh],
            gc_in.at[group],
            send_sem.at[1],
            recv_sem.at[1],
            ia,
            2 * dyh + core,
            dka,
        ).start()

    second_tr = transposed(second_ref[...])
    second_t[...] = second_tr.reshape(nia, q4, tj)
    gs_loc[...] = dot(second_tr.astype(BF16), second_ref[...]).reshape(slots, q1, rank)
    gs_in[ja] = gs_loc[slot1]

    @pl.loop(1, nja)
    def _(t):
        dja = wrap(ja + t, nja)
        remote(
            gs_loc.at[ka * nja + dja], gs_in.at[ja], send_sem.at[2], recv_sem.at[2], ia, dja, ka
        ).start()

    first_t[...] = transposed(first_ref[...]).reshape(slots, q1, ti)
    second_f[...] = second_ref[...].astype(F32)
    time_f[...] = time_ref[...].astype(F32)
    paired_sum(nia - 1)

    rows = lax.broadcasted_iota(jnp.int32, (256, 256), 0)
    columns = lax.broadcasted_iota(jnp.int32, (256, 256), 1)
    order = (lax.rem(rows, 16) == columns // 16) & (rows // 16 == lax.rem(columns, 16))
    order = order.astype(F32).astype(BF16)

    @pl.loop(0, ti // 16)
    def _(b):
        tens_copy(b).wait()
        i0 = pl.multiple_of(b * 16, 16)
        for c in range(half // 16):
            low = tens[pl.ds(i0, 16), 16 * c : 16 * c + 16, :].reshape(256, tk)
            high = tens[pl.ds(i0, 16), half + 16 * c : half + 16 * c + 16, :].reshape(256, tk)
            block = dot(order, jnp.concatenate([low, high], axis=1))
            perm[16 * c : 16 * c + 16, pl.ds(i0, 16), :] = block.astype(BF16).reshape(16, 16, 2 * tk)

    slab_acc[...] = jnp.zeros_like(slab_acc)

    @pl.loop(0, half // 4)
    def _(b):
        total = slab_acc[...]
        for u in range(4):
            j = b * 4 + u
            khatri = jnp.concatenate(
                [time_f[...] * second_f[pl.ds(j, 1), :], time_f[...] * second_f[pl.ds(j + half, 1), :]],
                axis=0,
            ).astype(BF16)
            total = total + dot(perm[j], khatri)
        slab_acc[...] = total

    slab_tr = slab_acc[...].T.reshape(groups, 2, q1, ti)
    slab_half[0] = slab_tr[:, 0]
    slab_half[1] = slab_tr[:, 1]
    slab_copy = remote(
        slab_half.at[other], slab_in, send_sem.at[4], recv_sem.at[4], ia, sibling, ka
    )
    slab_copy.start()

    unit = identity(2 * tk)

    def turn_blocks(start, stop):
        @pl.loop(start, stop)
        def _(b):
            for u in range(4):
                turn[4 * b + u] = dot_nt(unit, perm[4 * b + u]).astype(BF16)

    wait_bytes(gc_in.at[pl.ds(0, groups - 1)], recv_sem.at[1])
    ga_in[ia] = jnp.sum(gc_in[...], axis=0)

    @pl.loop(0, nia - 1)
    def _(t):
        remote(ga_in.at[ia], ga_in.at[ia], send_sem.at[5], recv_sem.at[5], ia_of(t), ja, ka).start()

    wait_bytes(gs_in.at[pl.ds(0, nja - 1)], recv_sem.at[2])
    wait_bytes(gt_in.at[pl.ds(0, nka - 1)], recv_sem.at[3])
    gram_part = jnp.sum(gs_in[...], axis=0) * jnp.sum(gt_in[...], axis=0)

    wait_bytes(ring_in, recv_sem.at[0])
    slab_copy.wait_recv()
    sum_half[...] = (
        coup[nia - 1, core] + jnp.sum(ring_in[...], axis=0) + (slab_half[core] + slab_in[...])
    )
    sum_in[group] = sum_half[group]

    @pl.loop(0, groups - 1)
    def _(t):
        dyh, dka = group_of(t)
        remote(
            sum_half.at[dka * nyh + dyh],
            sum_in.at[group],
            send_sem.at[6],
            recv_sem.at[6],
            ia,
            2 * dyh + core,
            dka,
        ).start()

    turn_blocks(0, half // 8)
    wait_bytes(ga_in.at[pl.ds(0, nia - 1)], recv_sem.at[5])
    gram_total = gram_part + jnp.sum(ga_in[...], axis=0)
    denominator = exact_product(gram_total, first_ref[...])
    wait_bytes(sum_in.at[pl.ds(0, groups - 1)], recv_sem.at[6])
    numerator = jnp.sum(sum_in[...], axis=0)
    fn_in[core, group] = (first_t[slot1] * numerator / denominator).astype(BF16)

    @pl.loop(0, groups - 1)
    def _(t):
        dyh, dka = group_of(t)
        remote(
            fn_in.at[core, group],
            fn_in.at[core, group],
            send_sem.at[7],
            recv_sem.at[7],
            ia,
            2 * dyh + core,
            dka,
        ).start()

    turn_blocks(half // 8, half // 4)
    wait_bytes(fn_in.at[0, pl.ds(0, groups - 1)], recv_sem.at[7])
    fn_copy = remote(fn_in.at[core], fn_in.at[core], send_sem.at[12], recv_sem.at[12], ia, sibling, ka)
    fn_copy.start()
    wait_bytes(gt_wide.at[pl.ds(0, nka - 1)], recv_sem.at[8])
    gt_rows = jnp.sum(gt_wide[...], axis=0).reshape(q4, rank)
    fn_copy.wait_recv()
    fn_t = jnp.stack([fn_in[0].astype(F32), fn_in[1].astype(F32)], axis=1)
    fn_t = fn_t.reshape(rank, ti).astype(BF16)
    fn = transposed(fn_t).astype(BF16)
    first_out[...] = fn
    gf_loc[...] = dot(fn_t, fn).reshape(nia, q4, rank)
    gf_in[ia] = gf_loc[ia]

    @pl.loop(0, nia - 1)
    def _(t):
        dia = ia_of(t)
        remote(gf_loc.at[dia], gf_in.at[ia], send_sem.at[16], recv_sem.at[16], dia, ja, ka).start()

    @pl.loop(0, half // 4)
    def _(b):
        for u in range(4):
            j = b * 4 + u
            block = dot(turn[j], first_out[...])
            wide[j] = block
            sums = jnp.sum(block.reshape(2, tk, rank) * time_f[...][None], axis=1)
            plane[pl.ds(j, 1), :] = sums[0:1]
            plane[pl.ds(j + half, 1), :] = sums[1:2]

    ps_loc[...] = plane[...].T.reshape(nia, q4, tj)
    ps_in[ia] = ps_loc[ia]

    @pl.loop(0, nia - 1)
    def _(t):
        dia = ia_of(t)
        remote(ps_loc.at[dia], ps_in.at[ia], send_sem.at[10], recv_sem.at[10], dia, ja, ka).start()

    wait_bytes(ps_in.at[pl.ds(0, nia - 1)], recv_sem.at[10])
    pa_in[ka] = jnp.sum(ps_in[...], axis=0)

    @pl.loop(0, nka - 1)
    def _(t):
        remote(pa_in.at[ka], pa_in.at[ka], send_sem.at[11], recv_sem.at[11], ia, ja, ka_of(t)).start()

    wait_bytes(gf_in.at[pl.ds(0, nia - 1)], recv_sem.at[16])
    gf_rows = jnp.sum(gf_in[...], axis=0)
    gf_sum[...] = gf_rows.reshape(nja, q3, rank)
    second_den = exact_product(gf_rows * gt_rows, second_ref[...])
    second_mine = second_t[ia]
    wait_bytes(pa_in.at[pl.ds(0, nka - 1)], recv_sem.at[11])
    second_num = jnp.sum(pa_in[...], axis=0)
    sn_in[ia] = (second_mine * second_num / second_den).astype(BF16)

    @pl.loop(0, nia - 1)
    def _(t):
        remote(sn_in.at[ia], sn_in.at[ia], send_sem.at[17], recv_sem.at[17], ia_of(t), ja, ka).start()

    wait_bytes(sn_in.at[pl.ds(0, nia - 1)], recv_sem.at[17])
    sn_t = sn_in[...].reshape(rank, tj)
    gn_loc[...] = dot_nt(sn_in[ia], sn_t).reshape(nja, q3, rank)
    gn_in[ja] = gn_loc[ja]

    @pl.loop(1, nja)
    def _(t):
        dja = wrap(ja + t, nja)
        remote(gn_loc.at[dja], gn_in.at[ja], send_sem.at[13], recv_sem.at[13], ia, dja, ka).start()

    sn_rows = transposed(sn_t)
    second_out[...] = sn_rows.astype(BF16)
    sn_f[...] = sn_rows

    def add_planes(b, total):
        for u in range(4):
            j = b * 4 + u
            total = total + wide[j, :tk] * sn_f[pl.ds(j, 1), :]
            total = total + wide[j, tk:] * sn_f[pl.ds(j + half, 1), :]
        return total

    tsum = lax.fori_loop(0, half // 4, add_planes, jnp.zeros((tk, rank), F32))
    ts_loc[...] = tsum.T.reshape(nia * nja, q3, tk)
    ts_in[slot3] = ts_loc[slot3]

    @pl.loop(0, nia * nja - 1)
    def _(t):
        dia, dja = plane_of(t)
        remote(
            ts_loc.at[dia * nja + dja], ts_in.at[slot3], send_sem.at[14], recv_sem.at[14], dia, dja, ka
        ).start()

    wait_bytes(gn_in.at[pl.ds(0, nja - 1)], recv_sem.at[13])
    gram_rows = gf_sum[ja] * jnp.sum(gn_in[...], axis=0)
    time_den = exact_product(gram_rows, time_ref[...])
    wait_bytes(ts_in.at[pl.ds(0, nia * nja - 1)], recv_sem.at[14])
    time_num = jnp.sum(ts_in[...], axis=0)
    tn_in[slot3] = (time_t[slot3] * time_num / time_den).astype(BF16)

    @pl.loop(0, nia * nja - 1)
    def _(t):
        dia, dja = plane_of(t)
        remote(
            tn_in.at[slot3], tn_in.at[slot3], send_sem.at[15], recv_sem.at[15], dia, dja, ka
        ).start()

    @pl.loop(0, nia)
    def _(s):
        pair_copy(s).wait_send()

    slab_copy.wait_send()
    gc_copy.wait_send()
    fn_copy.wait_send()
    for place_, ref in (
        (0, ring_in),
        (1, gc_in.at[pl.ds(0, groups - 1)]),
        (2, gs_in.at[pl.ds(0, nja - 1)]),
        (3, gt_in.at[pl.ds(0, nka - 1)]),
        (5, ga_in.at[pl.ds(0, nia - 1)]),
        (6, sum_in.at[pl.ds(0, groups - 1)]),
        (7, fn_in.at[0, pl.ds(0, groups - 1)]),
        (8, gt_wide.at[pl.ds(0, nka - 1)]),
        (10, ps_in.at[pl.ds(0, nia - 1)]),
        (11, pa_in.at[pl.ds(0, nka - 1)]),
        (13, gn_in.at[pl.ds(0, nja - 1)]),
        (14, ts_in.at[pl.ds(0, nia * nja - 1)]),
        (15, tn_in.at[pl.ds(0, nia * nja - 1)]),
        (16, gf_in.at[pl.ds(0, nia - 1)]),
        (17, sn_in.at[pl.ds(0, nia - 1)]),
    ):
        wait_bytes(ref, send_sem.at[place_])

    wait_bytes(tn_in.at[pl.ds(0, nia * nja - 1)], recv_sem.at[15])
    tn_t = tn_in[...].astype(F32).reshape(rank, tk).astype(BF16)
    time_out[...] = transposed(tn_t).astype(BF16)


def hand_out(first, second, time, first_out, second_out, time_out):
    first_out[...] = first[...]
    second_out[...] = second[...]
    time_out[...] = time[...]


def on_device(nia, nja, nka, tensor, matrix, first_factor, second_factor, time_factor, column_factor):
    ti, tj, tk = tensor.shape
    rank = first_factor.shape[1]
    depth = column_factor.shape[0]
    nyh = nja // 2
    slots = nja * nka
    q1, q3 = rank // slots, rank // (nia * nja)
    q4 = nja * q3
    groups = nka * nyh
    half = tj // 2
    V = pltpu.VMEM
    scratch = [
        V((ti, tj, tk), BF16),
        V((half, ti, 2 * tk), BF16),
        V((half, 2 * tk, ti), BF16),
        V((half, 2 * tk, rank), F32),
        V((nia, ti, depth), BF16),
        V((rank, depth), BF16),
        V((nia, 2, groups, q1, ti), F32),
        V((nia, groups, q1, ti), F32),
        V((nia - 1, groups, q1, ti), F32),
        V((ti, rank), F32),
        V((2, groups, q1, ti), F32),
        V((groups, q1, ti), F32),
        V((groups, q1, ti), F32),
        V((groups, q1, ti), F32),
        V((2, groups, q1, rank), F32),
        V((groups, q1, rank), F32),
        V((groups, q1, rank), F32),
        V((groups, q1, rank), F32),
        V((slots, q1, rank), F32),
        V((nja, q1, rank), F32),
        V((slots, q1, rank), F32),
        V((nka, q1, rank), F32),
        V((nka, q4 // q1, q1, rank), F32),
        V((nia, q1, rank), F32),
        V((slots, q1, ti), F32),
        V((nia, q4, tj), F32),
        V((nia * nja, q3, tk), F32),
        V((tj, rank), F32),
        V((tk, rank), F32),
        V((2, groups, q1, ti), BF16),
        V((nia, q4, rank), F32),
        V((nia, q4, rank), F32),
        V((nja, q3, rank), F32),
        V((tj, rank), F32),
        V((nia, q4, tj), F32),
        V((nia, q4, tj), F32),
        V((nka, q4, tj), F32),
        V((nia, q4, tj), BF16),
        V((nja, q3, rank), F32),
        V((nja, q3, rank), F32),
        V((tj, rank), F32),
        V((nia * nja, q3, tk), F32),
        V((nia * nja, q3, tk), F32),
        V((nia * nja, q3, tk), BF16),
        pltpu.SemaphoreType.DMA((nia,)),
        pltpu.SemaphoreType.DMA((ti // 16,)),
        pltpu.SemaphoreType.DMA((nia,)),
        pltpu.SemaphoreType.DMA((nia,)),
        pltpu.SemaphoreType.DMA((18,)),
        pltpu.SemaphoreType.DMA((18,)),
    ]
    in_vmem = pl.BlockSpec(memory_space=pltpu.VMEM)
    in_place = pl.BlockSpec(memory_space=pl.ANY)
    shapes = (
        jax.ShapeDtypeStruct((ti, rank), BF16),
        jax.ShapeDtypeStruct((tj, rank), BF16),
        jax.ShapeDtypeStruct((tk, rank), BF16),
    )
    results = pl.pallas_call(
        functools.partial(kernel, (nia, nja, nka, rank, ti, tj, tk)),
        out_shape=shapes,
        in_specs=[in_place, in_place, in_vmem, in_vmem, in_vmem, in_vmem],
        out_specs=(in_vmem, in_vmem, in_vmem),
        scratch_shapes=scratch,
        compiler_params=pltpu.CompilerParams(
            collective_id=0, has_side_effects=True, vmem_limit_bytes=60 * 1024 * 1024
        ),
        name="factor_round",
    )(tensor, matrix, first_factor, second_factor, time_factor, column_factor)
    return pl.pallas_call(
        hand_out,
        out_shape=shapes,
        in_specs=[in_vmem] * 3,
        out_specs=(in_vmem,) * 3,
        name="hand_out",
    )(*results)


def solution(mesh):
    sizes = (mesh.shape["ia"], mesh.shape["ja"], mesh.shape["ka"])
    return jax.shard_map(
        functools.partial(on_device, *sizes),
        mesh=mesh,
        in_specs=(
            P("ia", "ja", "ka"),
            P(None, ("ia", "ja", "ka")),
            P("ia", None),
            P("ja", None),
            P("ka", None),
            P(("ia", "ja", "ka"), None),
        ),
        out_specs=(P("ia", None), P("ja", None), P("ka", None)),
        check_vma=False,
    )
```

```python
import functools

import jax
import jax.numpy as jnp
from jax import lax
from jax.experimental import pallas as pl
from jax.experimental.pallas import tpu as pltpu
from jax.sharding import PartitionSpec as P

F32 = jnp.float32
BF16 = jnp.bfloat16


def dot(a, b):
    return jnp.dot(a, b, preferred_element_type=F32)


def dot_nt(a, b):
    return lax.dot_general(a, b, (((1,), (1,)), ((), ())), preferred_element_type=F32)


def identity(n):
    rows = lax.broadcasted_iota(jnp.int32, (n, n), 0)
    columns = lax.broadcasted_iota(jnp.int32, (n, n), 1)
    return (rows == columns).astype(F32).astype(BF16)


def transposed(values):
    return dot_nt(identity(values.shape[1]), values)


def exact_product(gram, factor):
    rows = gram.shape[0]
    high = gram.astype(BF16).astype(F32)
    rest = gram - high
    middle = rest.astype(BF16).astype(F32)
    low = (rest - middle).astype(BF16).astype(F32)
    parts = [high, middle, low]
    while (rows * len(parts)) % 16:
        parts.append(jnp.zeros_like(high))
    stacked = dot_nt(jnp.concatenate(parts, axis=0).astype(BF16), factor)
    return stacked[:rows] + (stacked[rows : 2 * rows] + stacked[2 * rows : 3 * rows])


def kernel(
    sizes,
    tensor_ref,
    matrix_ref,
    first_ref,
    second_ref,
    time_ref,
    column_ref,
    first_out,
    second_out,
    time_out,
    tens,
    perm,
    turn,
    wide,
    mats,
    col_t,
    coup,
    pair_in,
    ring_in,
    slab_acc,
    slab_half,
    slab_in,
    sum_half,
    sum_in,
    gc_loc,
    gc_pair,
    gc_half,
    gc_in,
    gs_loc,
    gs_in,
    gt_loc,
    gt_in,
    gt_wide,
    ga_in,
    first_t,
    second_t,
    time_t,
    second_f,
    time_f,
    fn_in,
    gf_loc,
    gf_in,
    gf_sum,
    plane,
    ps_loc,
    ps_in,
    pa_in,
    sn_in,
    gn_loc,
    gn_in,
    sn_f,
    ts_loc,
    ts_in,
    tn_in,
    mat_sem,
    tens_sem,
    pair_send,
    pair_recv,
    send_sem,
    recv_sem,
):
    nia, nja, nka, rank, ti, tj, tk = sizes
    nyh = nja // 2
    nx = nia // 2
    slots = nja * nka
    q1, q3 = rank // slots, rank // (nia * nja)
    q4 = nja * q3
    groups = nka * nyh
    half = tj // 2
    ia, ja, ka = lax.axis_index("ia"), lax.axis_index("ja"), lax.axis_index("ka")
    core = lax.rem(ja, 2)
    other = 1 - core
    yh = ja // 2
    slot1 = ka * nja + ja
    group = ka * nyh + yh
    slot3 = ia * nja + ja

    def wrap(value, n):
        return lax.rem(value + n, n)

    def far(u, n):
        return n // 2 + (1 - 2 * lax.rem(u, 2)) * ((u + 1) // 2)

    def ia_of(u):
        row = wrap(ia // nx + 1 - u // nx, 2)
        return row * nx + wrap(lax.rem(ia, nx) + far(lax.rem(u, nx), nx), nx)

    def ka_of(u):
        return wrap(ka + far(u, nka), nka)

    def group_of(t):
        return wrap(yh + nyh - 1 - lax.rem(t, nyh), nyh), ka_of(t // nyh)

    def plane_of(t):
        return ia_of(t // nja), wrap(ja + far(lax.rem(t, nja), nja), nja)

    def remote(src, dst, s_sem, r_sem, dia, dja, dka):
        return pltpu.make_async_remote_copy(
            src_ref=src,
            dst_ref=dst,
            send_sem=s_sem,
            recv_sem=r_sem,
            device_id=(dia, dja, dka),
            device_id_type=pl.DeviceIdType.MESH,
        )

    def wait_bytes(ref, sem):
        pltpu.make_async_copy(ref, ref, sem).wait()

    sibling = ja + 1 - 2 * core
    block_of = ia_of

    def mat_copy(s):
        rows = pl.ds(pl.multiple_of(block_of(s) * ti, ti), ti)
        return pltpu.make_async_copy(matrix_ref.at[rows, :], mats.at[s], mat_sem.at[s])

    def tens_copy(b):
        rows = pl.ds(b * 16, 16)
        return pltpu.make_async_copy(tensor_ref.at[rows], tens.at[rows], tens_sem.at[b])

    @pl.loop(0, nia)
    def _(s):
        mat_copy(s).start()

    @pl.loop(0, ti // 16)
    def _(b):
        tens_copy(b).start()

    barrier = pltpu.get_barrier_semaphore()

    def greet(dia, dja, dka):
        pl.semaphore_signal(
            barrier, inc=1, device_id=(dia, dja, dka), device_id_type=pl.DeviceIdType.MESH
        )

    @pl.loop(0, groups - 1)
    def _(t):
        dyh, dka = group_of(t)
        greet(ia, 2 * dyh + core, dka)

    @pl.loop(0, (nia - 1) * nja)
    def _(t):
        dia, dja = plane_of(t)
        greet(dia, dja, ka)

    greet(ia, 2 * (1 - yh) + other, ka)
    greet(ia, sibling, ka)
    col_t[...] = transposed(column_ref[...]).astype(BF16)

    def pair_copy(s):
        return remote(
            coup.at[s, other], pair_in.at[s], pair_send.at[s], pair_recv.at[s], ia, sibling, ka
        )

    def coupled_block(s):
        mat_copy(s).wait()
        block = dot_nt(col_t[...], mats[s]).reshape(groups, 2, q1, ti)
        coup[s, 0] = block[:, 0]
        coup[s, 1] = block[:, 1]

    def paired_sum(s):
        pair_copy(s).wait_recv()
        coup[s, core] = coup[s, core] + pair_in[s]

    def ring_copy(s):
        return remote(
            coup.at[s, core], ring_in.at[s], send_sem.at[0], recv_sem.at[0], block_of(s), ja, ka
        )

    @pl.loop(0, nia)
    def _(s):
        coupled_block(s)

    pl.semaphore_wait(barrier, groups - 1 + (nia - 1) * nja + 2)

    @pl.loop(0, nia)
    def _(s):
        pair_copy(s).start()

    gram = dot(col_t[...], column_ref[...]).reshape(groups, 2, q1, rank)
    gc_loc[0] = gram[:, 0]
    gc_loc[1] = gram[:, 1]
    gc_copy = remote(gc_loc.at[other], gc_pair, send_sem.at[9], recv_sem.at[9], ia, sibling, ka)
    gc_copy.start()

    @pl.loop(0, nia - 1)
    def _(s):
        paired_sum(s)
        ring_copy(s).start()

    time_tr = transposed(time_ref[...])
    time_t[...] = time_tr.reshape(nia * nja, q3, tk)
    gt_loc[...] = dot(time_tr.astype(BF16), time_ref[...]).reshape(slots, q1, rank)
    mine = pl.ds(ia * (q4 // q1), q4 // q1)
    gt_in[ka] = gt_loc[slot1]
    gt_wide[ka] = gt_loc[mine]

    @pl.loop(0, nka - 1)
    def _(t):
        dka = ka_of(t)
        remote(
            gt_loc.at[dka * nja + ja], gt_in.at[ka], send_sem.at[3], recv_sem.at[3], ia, ja, dka
        ).start()
        remote(gt_loc.at[mine], gt_wide.at[ka], send_sem.at[8], recv_sem.at[8], ia, ja, dka).start()

    gc_copy.wait_recv()
    gc_half[...] = gc_loc[core] + gc_pair[...]
    gc_in[group] = gc_half[group]

    @pl.loop(0, groups - 1)
    def _(t):
        dyh, dka = group_of(t)
        remote(
            gc_half.at[dka * nyh + dyh],
            gc_in.at[group],
            send_sem.at[1],
            recv_sem.at[1],
            ia,
            2 * dyh + core,
            dka,
        ).start()

    second_tr = transposed(second_ref[...])
    second_t[...] = second_tr.reshape(nia, q4, tj)
    gs_loc[...] = dot(second_tr.astype(BF16), second_ref[...]).reshape(slots, q1, rank)
    gs_in[ja] = gs_loc[slot1]

    @pl.loop(1, nja)
    def _(t):
        dja = wrap(ja + t, nja)
        remote(
            gs_loc.at[ka * nja + dja], gs_in.at[ja], send_sem.at[2], recv_sem.at[2], ia, dja, ka
        ).start()

    first_t[...] = transposed(first_ref[...]).reshape(slots, q1, ti)
    second_f[...] = second_ref[...].astype(F32)
    time_f[...] = time_ref[...].astype(F32)
    paired_sum(nia - 1)

    rows = lax.broadcasted_iota(jnp.int32, (256, 256), 0)
    columns = lax.broadcasted_iota(jnp.int32, (256, 256), 1)
    order = (lax.rem(rows, 16) == columns // 16) & (rows // 16 == lax.rem(columns, 16))
    order = order.astype(F32).astype(BF16)

    @pl.loop(0, ti // 16)
    def _(b):
        tens_copy(b).wait()
        i0 = pl.multiple_of(b * 16, 16)
        for c in range(half // 16):
            low = tens[pl.ds(i0, 16), 16 * c : 16 * c + 16, :].reshape(256, tk)
            high = tens[pl.ds(i0, 16), half + 16 * c : half + 16 * c + 16, :].reshape(256, tk)
            block = dot(order, jnp.concatenate([low, high], axis=1))
            perm[16 * c : 16 * c + 16, pl.ds(i0, 16), :] = block.astype(BF16).reshape(16, 16, 2 * tk)

    slab_acc[...] = jnp.zeros_like(slab_acc)

    @pl.loop(0, half // 4)
    def _(b):
        total = slab_acc[...]
        for u in range(4):
            j = b * 4 + u
            khatri = jnp.concatenate(
                [time_f[...] * second_f[pl.ds(j, 1), :], time_f[...] * second_f[pl.ds(j + half, 1), :]],
                axis=0,
            ).astype(BF16)
            total = total + dot(perm[j], khatri)
        slab_acc[...] = total

    slab_tr = slab_acc[...].T.reshape(groups, 2, q1, ti)
    slab_half[0] = slab_tr[:, 0]
    slab_half[1] = slab_tr[:, 1]
    slab_copy = remote(
        slab_half.at[other], slab_in, send_sem.at[4], recv_sem.at[4], ia, sibling, ka
    )
    slab_copy.start()

    unit = identity(2 * tk)

    def turn_blocks(start, stop):
        @pl.loop(start, stop)
        def _(b):
            for u in range(4):
                turn[4 * b + u] = dot_nt(unit, perm[4 * b + u]).astype(BF16)

    wait_bytes(gc_in.at[pl.ds(0, groups - 1)], recv_sem.at[1])
    ga_in[ia] = jnp.sum(gc_in[...], axis=0)

    @pl.loop(0, nia - 1)
    def _(t):
        remote(ga_in.at[ia], ga_in.at[ia], send_sem.at[5], recv_sem.at[5], ia_of(t), ja, ka).start()

    wait_bytes(gs_in.at[pl.ds(0, nja - 1)], recv_sem.at[2])
    wait_bytes(gt_in.at[pl.ds(0, nka - 1)], recv_sem.at[3])
    gram_part = jnp.sum(gs_in[...], axis=0) * jnp.sum(gt_in[...], axis=0)

    wait_bytes(ring_in, recv_sem.at[0])
    slab_copy.wait_recv()
    sum_half[...] = (
        coup[nia - 1, core] + jnp.sum(ring_in[...], axis=0) + (slab_half[core] + slab_in[...])
    )
    sum_in[group] = sum_half[group]

    @pl.loop(0, groups - 1)
    def _(t):
        dyh, dka = group_of(t)
        remote(
            sum_half.at[dka * nyh + dyh],
            sum_in.at[group],
            send_sem.at[6],
            recv_sem.at[6],
            ia,
            2 * dyh + core,
            dka,
        ).start()

    turn_blocks(0, half // 8)
    wait_bytes(ga_in.at[pl.ds(0, nia - 1)], recv_sem.at[5])
    gram_total = gram_part + jnp.sum(ga_in[...], axis=0)
    denominator = exact_product(gram_total, first_ref[...])
    wait_bytes(sum_in.at[pl.ds(0, groups - 1)], recv_sem.at[6])
    numerator = jnp.sum(sum_in[...], axis=0)
    fn_in[core, group] = (first_t[slot1] * numerator / denominator).astype(BF16)

    @pl.loop(0, groups - 1)
    def _(t):
        dyh, dka = group_of(t)
        remote(
            fn_in.at[core, group],
            fn_in.at[core, group],
            send_sem.at[7],
            recv_sem.at[7],
            ia,
            2 * dyh + core,
            dka,
        ).start()

    turn_blocks(half // 8, half // 4)
    wait_bytes(fn_in.at[0, pl.ds(0, groups - 1)], recv_sem.at[7])
    fn_copy = remote(fn_in.at[core], fn_in.at[core], send_sem.at[12], recv_sem.at[12], ia, sibling, ka)
    fn_copy.start()
    fn_copy.wait_recv()
    fn_t = jnp.stack([fn_in[0].astype(F32), fn_in[1].astype(F32)], axis=1)
    fn_t = fn_t.reshape(rank, ti).astype(BF16)
    fn = transposed(fn_t).astype(BF16)
    first_out[...] = fn
    @pl.loop(0, half // 8)
    def _(b):
        for u in range(8):
            j = b * 8 + u
            block = dot(turn[j], first_out[...])
            wide[j] = block
            sums = jnp.sum(block.reshape(2, tk, rank) * time_f[...][None], axis=1)
            plane[pl.ds(j, 1), :] = sums[0:1]
            plane[pl.ds(j + half, 1), :] = sums[1:2]

    ps_loc[...] = plane[...].T.reshape(nia, q4, tj)
    ps_in[ia] = ps_loc[ia]

    @pl.loop(0, nia - 1)
    def _(t):
        dia = ia_of(t)
        remote(ps_loc.at[dia], ps_in.at[ia], send_sem.at[10], recv_sem.at[10], dia, ja, ka).start()

    gf_loc[...] = dot(fn_t, first_out[...]).reshape(nia, q4, rank)
    gf_in[ia] = gf_loc[ia]

    @pl.loop(0, nia - 1)
    def _(t):
        dia = ia_of(t)
        remote(gf_loc.at[dia], gf_in.at[ia], send_sem.at[16], recv_sem.at[16], dia, ja, ka).start()

    wait_bytes(gt_wide.at[pl.ds(0, nka - 1)], recv_sem.at[8])
    gt_rows = jnp.sum(gt_wide[...], axis=0).reshape(q4, rank)
    wait_bytes(ps_in.at[pl.ds(0, nia - 1)], recv_sem.at[10])
    pa_in[ka] = jnp.sum(ps_in[...], axis=0)

    @pl.loop(0, nka - 1)
    def _(t):
        remote(pa_in.at[ka], pa_in.at[ka], send_sem.at[11], recv_sem.at[11], ia, ja, ka_of(t)).start()

    wait_bytes(gf_in.at[pl.ds(0, nia - 1)], recv_sem.at[16])
    gf_rows = jnp.sum(gf_in[...], axis=0)
    gf_sum[...] = gf_rows.reshape(nja, q3, rank)
    second_den = exact_product(gf_rows * gt_rows, second_ref[...])
    second_mine = second_t[ia]
    wait_bytes(pa_in.at[pl.ds(0, nka - 1)], recv_sem.at[11])
    second_num = jnp.sum(pa_in[...], axis=0)
    sn_in[ia] = (second_mine * second_num / second_den).astype(BF16)

    @pl.loop(0, nia - 1)
    def _(t):
        remote(sn_in.at[ia], sn_in.at[ia], send_sem.at[17], recv_sem.at[17], ia_of(t), ja, ka).start()

    wait_bytes(sn_in.at[pl.ds(0, nia - 1)], recv_sem.at[17])
    sn_t = sn_in[...].reshape(rank, tj)
    gn_loc[...] = dot_nt(sn_in[ia], sn_t).reshape(nja, q3, rank)
    gn_in[ja] = gn_loc[ja]

    @pl.loop(1, nja)
    def _(t):
        dja = wrap(ja + t, nja)
        remote(gn_loc.at[dja], gn_in.at[ja], send_sem.at[13], recv_sem.at[13], ia, dja, ka).start()

    sn_rows = transposed(sn_t)
    second_out[...] = sn_rows.astype(BF16)
    sn_f[...] = sn_rows

    def add_planes(b, total):
        for u in range(4):
            j = b * 4 + u
            total = total + wide[j, :tk] * sn_f[pl.ds(j, 1), :]
            total = total + wide[j, tk:] * sn_f[pl.ds(j + half, 1), :]
        return total

    tsum = lax.fori_loop(0, half // 4, add_planes, jnp.zeros((tk, rank), F32))
    ts_loc[...] = tsum.T.reshape(nia * nja, q3, tk)
    ts_in[slot3] = ts_loc[slot3]

    @pl.loop(0, nia * nja - 1)
    def _(t):
        dia, dja = plane_of(t)
        remote(
            ts_loc.at[dia * nja + dja], ts_in.at[slot3], send_sem.at[14], recv_sem.at[14], dia, dja, ka
        ).start()

    wait_bytes(gn_in.at[pl.ds(0, nja - 1)], recv_sem.at[13])
    gram_rows = gf_sum[ja] * jnp.sum(gn_in[...], axis=0)
    time_den = exact_product(gram_rows, time_ref[...])
    wait_bytes(ts_in.at[pl.ds(0, nia * nja - 1)], recv_sem.at[14])
    time_num = jnp.sum(ts_in[...], axis=0)
    tn_in[slot3] = (time_t[slot3] * time_num / time_den).astype(BF16)

    @pl.loop(0, nia * nja - 1)
    def _(t):
        dia, dja = plane_of(t)
        remote(
            tn_in.at[slot3], tn_in.at[slot3], send_sem.at[15], recv_sem.at[15], dia, dja, ka
        ).start()

    @pl.loop(0, nia)
    def _(s):
        pair_copy(s).wait_send()

    slab_copy.wait_send()
    gc_copy.wait_send()
    fn_copy.wait_send()
    for place_, ref in (
        (0, ring_in),
        (1, gc_in.at[pl.ds(0, groups - 1)]),
        (2, gs_in.at[pl.ds(0, nja - 1)]),
        (3, gt_in.at[pl.ds(0, nka - 1)]),
        (5, ga_in.at[pl.ds(0, nia - 1)]),
        (6, sum_in.at[pl.ds(0, groups - 1)]),
        (7, fn_in.at[0, pl.ds(0, groups - 1)]),
        (8, gt_wide.at[pl.ds(0, nka - 1)]),
        (10, ps_in.at[pl.ds(0, nia - 1)]),
        (11, pa_in.at[pl.ds(0, nka - 1)]),
        (13, gn_in.at[pl.ds(0, nja - 1)]),
        (14, ts_in.at[pl.ds(0, nia * nja - 1)]),
        (15, tn_in.at[pl.ds(0, nia * nja - 1)]),
        (16, gf_in.at[pl.ds(0, nia - 1)]),
        (17, sn_in.at[pl.ds(0, nia - 1)]),
    ):
        wait_bytes(ref, send_sem.at[place_])

    wait_bytes(tn_in.at[pl.ds(0, nia * nja - 1)], recv_sem.at[15])
    tn_t = tn_in[...].astype(F32).reshape(rank, tk).astype(BF16)
    time_out[...] = transposed(tn_t).astype(BF16)


def hand_out(first, second, time, first_out, second_out, time_out):
    first_out[...] = first[...]
    second_out[...] = second[...]
    time_out[...] = time[...]


def on_device(nia, nja, nka, tensor, matrix, first_factor, second_factor, time_factor, column_factor):
    ti, tj, tk = tensor.shape
    rank = first_factor.shape[1]
    depth = column_factor.shape[0]
    nyh = nja // 2
    slots = nja * nka
    q1, q3 = rank // slots, rank // (nia * nja)
    q4 = nja * q3
    groups = nka * nyh
    half = tj // 2
    V = pltpu.VMEM
    scratch = [
        V((ti, tj, tk), BF16),
        V((half, ti, 2 * tk), BF16),
        V((half, 2 * tk, ti), BF16),
        V((half, 2 * tk, rank), F32),
        V((nia, ti, depth), BF16),
        V((rank, depth), BF16),
        V((nia, 2, groups, q1, ti), F32),
        V((nia, groups, q1, ti), F32),
        V((nia - 1, groups, q1, ti), F32),
        V((ti, rank), F32),
        V((2, groups, q1, ti), F32),
        V((groups, q1, ti), F32),
        V((groups, q1, ti), F32),
        V((groups, q1, ti), F32),
        V((2, groups, q1, rank), F32),
        V((groups, q1, rank), F32),
        V((groups, q1, rank), F32),
        V((groups, q1, rank), F32),
        V((slots, q1, rank), F32),
        V((nja, q1, rank), F32),
        V((slots, q1, rank), F32),
        V((nka, q1, rank), F32),
        V((nka, q4 // q1, q1, rank), F32),
        V((nia, q1, rank), F32),
        V((slots, q1, ti), F32),
        V((nia, q4, tj), F32),
        V((nia * nja, q3, tk), F32),
        V((tj, rank), F32),
        V((tk, rank), F32),
        V((2, groups, q1, ti), BF16),
        V((nia, q4, rank), F32),
        V((nia, q4, rank), F32),
        V((nja, q3, rank), F32),
        V((tj, rank), F32),
        V((nia, q4, tj), F32),
        V((nia, q4, tj), F32),
        V((nka, q4, tj), F32),
        V((nia, q4, tj), BF16),
        V((nja, q3, rank), F32),
        V((nja, q3, rank), F32),
        V((tj, rank), F32),
        V((nia * nja, q3, tk), F32),
        V((nia * nja, q3, tk), F32),
        V((nia * nja, q3, tk), BF16),
        pltpu.SemaphoreType.DMA((nia,)),
        pltpu.SemaphoreType.DMA((ti // 16,)),
        pltpu.SemaphoreType.DMA((nia,)),
        pltpu.SemaphoreType.DMA((nia,)),
        pltpu.SemaphoreType.DMA((18,)),
        pltpu.SemaphoreType.DMA((18,)),
    ]
    in_vmem = pl.BlockSpec(memory_space=pltpu.VMEM)
    in_place = pl.BlockSpec(memory_space=pl.ANY)
    shapes = (
        jax.ShapeDtypeStruct((ti, rank), BF16),
        jax.ShapeDtypeStruct((tj, rank), BF16),
        jax.ShapeDtypeStruct((tk, rank), BF16),
    )
    results = pl.pallas_call(
        functools.partial(kernel, (nia, nja, nka, rank, ti, tj, tk)),
        out_shape=shapes,
        in_specs=[in_place, in_place, in_vmem, in_vmem, in_vmem, in_vmem],
        out_specs=(in_vmem, in_vmem, in_vmem),
        scratch_shapes=scratch,
        compiler_params=pltpu.CompilerParams(
            collective_id=0, has_side_effects=True, vmem_limit_bytes=60 * 1024 * 1024
        ),
        name="factor_round",
    )(tensor, matrix, first_factor, second_factor, time_factor, column_factor)
    return pl.pallas_call(
        hand_out,
        out_shape=shapes,
        in_specs=[in_vmem] * 3,
        out_specs=(in_vmem,) * 3,
        name="hand_out",
    )(*results)


def solution(mesh):
    sizes = (mesh.shape["ia"], mesh.shape["ja"], mesh.shape["ka"])
    return jax.shard_map(
        functools.partial(on_device, *sizes),
        mesh=mesh,
        in_specs=(
            P("ia", "ja", "ka"),
            P(None, ("ia", "ja", "ka")),
            P("ia", None),
            P("ja", None),
            P("ka", None),
            P(("ia", "ja", "ka"), None),
        ),
        out_specs=(P("ia", None), P("ja", None), P("ka", None)),
        check_vma=False,
    )
```

```python
import functools

import jax
import jax.numpy as jnp
from jax import lax
from jax.experimental import pallas as pl
from jax.experimental.pallas import tpu as pltpu
from jax.sharding import PartitionSpec as P

F32 = jnp.float32
BF16 = jnp.bfloat16


def dot(a, b):
    return jnp.dot(a, b, preferred_element_type=F32)


def dot_nt(a, b):
    return lax.dot_general(a, b, (((1,), (1,)), ((), ())), preferred_element_type=F32)


def identity(n):
    rows = lax.broadcasted_iota(jnp.int32, (n, n), 0)
    columns = lax.broadcasted_iota(jnp.int32, (n, n), 1)
    return (rows == columns).astype(F32).astype(BF16)


def transposed(values):
    return dot_nt(identity(values.shape[1]), values)


def exact_product(gram, factor):
    rows = gram.shape[0]
    high = gram.astype(BF16).astype(F32)
    rest = gram - high
    middle = rest.astype(BF16).astype(F32)
    low = (rest - middle).astype(BF16).astype(F32)
    parts = [high, middle, low]
    while (rows * len(parts)) % 16:
        parts.append(jnp.zeros_like(high))
    stacked = dot_nt(jnp.concatenate(parts, axis=0).astype(BF16), factor)
    return stacked[:rows] + (stacked[rows : 2 * rows] + stacked[2 * rows : 3 * rows])


def kernel(
    sizes,
    tensor_ref,
    matrix_ref,
    first_ref,
    second_ref,
    time_ref,
    column_ref,
    first_out,
    second_out,
    time_out,
    tens,
    perm,
    turn,
    wide,
    mats,
    col_t,
    coup,
    pair_in,
    ring_in,
    slab_acc,
    slab_half,
    slab_in,
    sum_half,
    sum_in,
    gc_loc,
    gc_pair,
    gc_half,
    gc_in,
    gs_loc,
    gs_in,
    gt_loc,
    gt_in,
    gt_wide,
    ga_in,
    first_t,
    second_t,
    time_t,
    second_f,
    time_f,
    fn_in,
    gf_loc,
    gf_in,
    gf_sum,
    plane,
    ps_loc,
    ps_in,
    pa_in,
    sn_in,
    gn_loc,
    gn_in,
    sn_f,
    ts_loc,
    ts_in,
    tn_in,
    mat_sem,
    tens_sem,
    pair_send,
    pair_recv,
    send_sem,
    recv_sem,
):
    nia, nja, nka, rank, ti, tj, tk = sizes
    nyh = nja // 2
    nx = nia // 2
    slots = nja * nka
    q1, q3 = rank // slots, rank // (nia * nja)
    q4 = nja * q3
    groups = nka * nyh
    half = tj // 2
    ia, ja, ka = lax.axis_index("ia"), lax.axis_index("ja"), lax.axis_index("ka")
    core = lax.rem(ja, 2)
    other = 1 - core
    yh = ja // 2
    slot1 = ka * nja + ja
    group = ka * nyh + yh
    slot3 = ia * nja + ja

    def wrap(value, n):
        return lax.rem(value + n, n)

    def far(u, n):
        return n // 2 + (1 - 2 * lax.rem(u, 2)) * ((u + 1) // 2)

    def ia_of(u):
        row = wrap(ia // nx + 1 - u // nx, 2)
        return row * nx + wrap(lax.rem(ia, nx) + far(lax.rem(u, nx), nx), nx)

    def ka_of(u):
        return wrap(ka + far(u, nka), nka)

    def group_of(t):
        return wrap(yh + nyh - 1 - lax.rem(t, nyh), nyh), ka_of(t // nyh)

    def plane_of(t):
        return ia_of(t // nja), wrap(ja + far(lax.rem(t, nja), nja), nja)

    def remote(src, dst, s_sem, r_sem, dia, dja, dka):
        return pltpu.make_async_remote_copy(
            src_ref=src,
            dst_ref=dst,
            send_sem=s_sem,
            recv_sem=r_sem,
            device_id=(dia, dja, dka),
            device_id_type=pl.DeviceIdType.MESH,
        )

    def wait_bytes(ref, sem):
        pltpu.make_async_copy(ref, ref, sem).wait()

    sibling = ja + 1 - 2 * core
    block_of = ia_of

    def mat_copy(s):
        rows = pl.ds(pl.multiple_of(block_of(s) * ti, ti), ti)
        return pltpu.make_async_copy(matrix_ref.at[rows, :], mats.at[s], mat_sem.at[s])

    def tens_copy(b):
        rows = pl.ds(b * 16, 16)
        return pltpu.make_async_copy(tensor_ref.at[rows], tens.at[rows], tens_sem.at[b])

    barrier = pltpu.get_barrier_semaphore()

    def greet(dia, dja, dka):
        pl.semaphore_signal(
            barrier, inc=1, device_id=(dia, dja, dka), device_id_type=pl.DeviceIdType.MESH
        )

    @pl.loop(0, groups - 1)
    def _(t):
        dyh, dka = group_of(t)
        greet(ia, 2 * dyh + core, dka)

    @pl.loop(0, (nia - 1) * nja)
    def _(t):
        dia, dja = plane_of(t)
        greet(dia, dja, ka)

    greet(ia, 2 * (1 - yh) + other, ka)
    greet(ia, sibling, ka)
    @pl.loop(0, nia)
    def _(s):
        mat_copy(s).start()

    @pl.loop(0, ti // 16)
    def _(b):
        tens_copy(b).start()

    col_t[...] = transposed(column_ref[...]).astype(BF16)

    def pair_copy(s):
        return remote(
            coup.at[s, other], pair_in.at[s], pair_send.at[s], pair_recv.at[s], ia, sibling, ka
        )

    def coupled_block(s):
        mat_copy(s).wait()
        block = dot_nt(col_t[...], mats[s]).reshape(groups, 2, q1, ti)
        coup[s, 0] = block[:, 0]
        coup[s, 1] = block[:, 1]

    def paired_sum(s):
        pair_copy(s).wait_recv()
        coup[s, core] = coup[s, core] + pair_in[s]

    def ring_copy(s):
        return remote(
            coup.at[s, core], ring_in.at[s], send_sem.at[0], recv_sem.at[0], block_of(s), ja, ka
        )

    @pl.loop(0, nia)
    def _(s):
        coupled_block(s)

    pl.semaphore_wait(barrier, groups - 1 + (nia - 1) * nja + 2)

    @pl.loop(0, nia)
    def _(s):
        pair_copy(s).start()

    gram = dot(col_t[...], column_ref[...]).reshape(groups, 2, q1, rank)
    gc_loc[0] = gram[:, 0]
    gc_loc[1] = gram[:, 1]
    gc_copy = remote(gc_loc.at[other], gc_pair, send_sem.at[9], recv_sem.at[9], ia, sibling, ka)
    gc_copy.start()

    @pl.loop(0, nia - 1)
    def _(s):
        paired_sum(s)
        ring_copy(s).start()

    time_tr = transposed(time_ref[...])
    time_t[...] = time_tr.reshape(nia * nja, q3, tk)
    gt_loc[...] = dot(time_tr.astype(BF16), time_ref[...]).reshape(slots, q1, rank)
    mine = pl.ds(ia * (q4 // q1), q4 // q1)
    gt_in[ka] = gt_loc[slot1]
    gt_wide[ka] = gt_loc[mine]

    @pl.loop(0, nka - 1)
    def _(t):
        dka = ka_of(t)
        remote(
            gt_loc.at[dka * nja + ja], gt_in.at[ka], send_sem.at[3], recv_sem.at[3], ia, ja, dka
        ).start()
        remote(gt_loc.at[mine], gt_wide.at[ka], send_sem.at[8], recv_sem.at[8], ia, ja, dka).start()

    gc_copy.wait_recv()
    gc_half[...] = gc_loc[core] + gc_pair[...]
    gc_in[group] = gc_half[group]

    @pl.loop(0, groups - 1)
    def _(t):
        dyh, dka = group_of(t)
        remote(
            gc_half.at[dka * nyh + dyh],
            gc_in.at[group],
            send_sem.at[1],
            recv_sem.at[1],
            ia,
            2 * dyh + core,
            dka,
        ).start()

    second_tr = transposed(second_ref[...])
    second_t[...] = second_tr.reshape(nia, q4, tj)
    gs_loc[...] = dot(second_tr.astype(BF16), second_ref[...]).reshape(slots, q1, rank)
    gs_in[ja] = gs_loc[slot1]

    @pl.loop(1, nja)
    def _(t):
        dja = wrap(ja + t, nja)
        remote(
            gs_loc.at[ka * nja + dja], gs_in.at[ja], send_sem.at[2], recv_sem.at[2], ia, dja, ka
        ).start()

    first_t[...] = transposed(first_ref[...]).reshape(slots, q1, ti)
    second_f[...] = second_ref[...].astype(F32)
    time_f[...] = time_ref[...].astype(F32)
    paired_sum(nia - 1)

    rows = lax.broadcasted_iota(jnp.int32, (256, 256), 0)
    columns = lax.broadcasted_iota(jnp.int32, (256, 256), 1)
    order = (lax.rem(rows, 16) == columns // 16) & (rows // 16 == lax.rem(columns, 16))
    order = order.astype(F32).astype(BF16)

    @pl.loop(0, ti // 16)
    def _(b):
        tens_copy(b).wait()
        i0 = pl.multiple_of(b * 16, 16)
        for c in range(half // 16):
            low = tens[pl.ds(i0, 16), 16 * c : 16 * c + 16, :].reshape(256, tk)
            high = tens[pl.ds(i0, 16), half + 16 * c : half + 16 * c + 16, :].reshape(256, tk)
            block = dot(order, jnp.concatenate([low, high], axis=1))
            perm[16 * c : 16 * c + 16, pl.ds(i0, 16), :] = block.astype(BF16).reshape(16, 16, 2 * tk)

    slab_acc[...] = jnp.zeros_like(slab_acc)

    @pl.loop(0, half // 4)
    def _(b):
        total = slab_acc[...]
        for u in range(4):
            j = b * 4 + u
            khatri = jnp.concatenate(
                [time_f[...] * second_f[pl.ds(j, 1), :], time_f[...] * second_f[pl.ds(j + half, 1), :]],
                axis=0,
            ).astype(BF16)
            total = total + dot(perm[j], khatri)
        slab_acc[...] = total

    slab_tr = slab_acc[...].T.reshape(groups, 2, q1, ti)
    slab_half[0] = slab_tr[:, 0]
    slab_half[1] = slab_tr[:, 1]
    slab_copy = remote(
        slab_half.at[other], slab_in, send_sem.at[4], recv_sem.at[4], ia, sibling, ka
    )
    slab_copy.start()

    unit = identity(2 * tk)

    def turn_blocks(start, stop):
        @pl.loop(start, stop)
        def _(b):
            for u in range(4):
                turn[4 * b + u] = dot_nt(unit, perm[4 * b + u]).astype(BF16)

    wait_bytes(gc_in.at[pl.ds(0, groups - 1)], recv_sem.at[1])
    ga_in[ia] = jnp.sum(gc_in[...], axis=0)

    @pl.loop(0, nia - 1)
    def _(t):
        remote(ga_in.at[ia], ga_in.at[ia], send_sem.at[5], recv_sem.at[5], ia_of(t), ja, ka).start()

    wait_bytes(gs_in.at[pl.ds(0, nja - 1)], recv_sem.at[2])
    wait_bytes(gt_in.at[pl.ds(0, nka - 1)], recv_sem.at[3])
    gram_part = jnp.sum(gs_in[...], axis=0) * jnp.sum(gt_in[...], axis=0)

    wait_bytes(ring_in, recv_sem.at[0])
    slab_copy.wait_recv()
    sum_half[...] = (
        coup[nia - 1, core] + jnp.sum(ring_in[...], axis=0) + (slab_half[core] + slab_in[...])
    )
    sum_in[group] = sum_half[group]

    @pl.loop(0, groups - 1)
    def _(t):
        dyh, dka = group_of(t)
        remote(
            sum_half.at[dka * nyh + dyh],
            sum_in.at[group],
            send_sem.at[6],
            recv_sem.at[6],
            ia,
            2 * dyh + core,
            dka,
        ).start()

    turn_blocks(0, half // 8)
    wait_bytes(ga_in.at[pl.ds(0, nia - 1)], recv_sem.at[5])
    gram_total = gram_part + jnp.sum(ga_in[...], axis=0)
    denominator = exact_product(gram_total, first_ref[...])
    wait_bytes(sum_in.at[pl.ds(0, groups - 1)], recv_sem.at[6])
    numerator = jnp.sum(sum_in[...], axis=0)
    fn_in[core, group] = (first_t[slot1] * numerator / denominator).astype(BF16)

    @pl.loop(0, groups - 1)
    def _(t):
        dyh, dka = group_of(t)
        remote(
            fn_in.at[core, group],
            fn_in.at[core, group],
            send_sem.at[7],
            recv_sem.at[7],
            ia,
            2 * dyh + core,
            dka,
        ).start()

    turn_blocks(half // 8, half // 4)
    wait_bytes(fn_in.at[0, pl.ds(0, groups - 1)], recv_sem.at[7])
    fn_copy = remote(fn_in.at[core], fn_in.at[core], send_sem.at[12], recv_sem.at[12], ia, sibling, ka)
    fn_copy.start()
    fn_copy.wait_recv()
    fn_t = jnp.stack([fn_in[0].astype(F32), fn_in[1].astype(F32)], axis=1)
    fn_t = fn_t.reshape(rank, ti).astype(BF16)
    fn = transposed(fn_t).astype(BF16)
    first_out[...] = fn
    @pl.loop(0, half // 8)
    def _(b):
        for u in range(8):
            j = b * 8 + u
            block = dot(turn[j], first_out[...])
            wide[j] = block
            sums = jnp.sum(block.reshape(2, tk, rank) * time_f[...][None], axis=1)
            plane[pl.ds(j, 1), :] = sums[0:1]
            plane[pl.ds(j + half, 1), :] = sums[1:2]

    ps_loc[...] = plane[...].T.reshape(nia, q4, tj)
    ps_in[ia] = ps_loc[ia]

    @pl.loop(0, nia - 1)
    def _(t):
        dia = ia_of(t)
        remote(ps_loc.at[dia], ps_in.at[ia], send_sem.at[10], recv_sem.at[10], dia, ja, ka).start()

    gf_loc[...] = dot(fn_t, first_out[...]).reshape(nia, q4, rank)
    gf_in[ia] = gf_loc[ia]

    @pl.loop(0, nia - 1)
    def _(t):
        dia = ia_of(t)
        remote(gf_loc.at[dia], gf_in.at[ia], send_sem.at[16], recv_sem.at[16], dia, ja, ka).start()

    wait_bytes(gt_wide.at[pl.ds(0, nka - 1)], recv_sem.at[8])
    gt_rows = jnp.sum(gt_wide[...], axis=0).reshape(q4, rank)
    wait_bytes(ps_in.at[pl.ds(0, nia - 1)], recv_sem.at[10])
    pa_in[ka] = jnp.sum(ps_in[...], axis=0)

    @pl.loop(0, nka - 1)
    def _(t):
        remote(pa_in.at[ka], pa_in.at[ka], send_sem.at[11], recv_sem.at[11], ia, ja, ka_of(t)).start()

    wait_bytes(gf_in.at[pl.ds(0, nia - 1)], recv_sem.at[16])
    gf_rows = jnp.sum(gf_in[...], axis=0)
    gf_sum[...] = gf_rows.reshape(nja, q3, rank)
    second_den = exact_product(gf_rows * gt_rows, second_ref[...])
    second_mine = second_t[ia]
    wait_bytes(pa_in.at[pl.ds(0, nka - 1)], recv_sem.at[11])
    second_num = jnp.sum(pa_in[...], axis=0)
    sn_in[ia] = (second_mine * second_num / second_den).astype(BF16)

    @pl.loop(0, nia - 1)
    def _(t):
        remote(sn_in.at[ia], sn_in.at[ia], send_sem.at[17], recv_sem.at[17], ia_of(t), ja, ka).start()

    wait_bytes(sn_in.at[pl.ds(0, nia - 1)], recv_sem.at[17])
    sn_t = sn_in[...].reshape(rank, tj)
    gn_loc[...] = dot_nt(sn_in[ia], sn_t).reshape(nja, q3, rank)
    gn_in[ja] = gn_loc[ja]

    @pl.loop(1, nja)
    def _(t):
        dja = wrap(ja + t, nja)
        remote(gn_loc.at[dja], gn_in.at[ja], send_sem.at[13], recv_sem.at[13], ia, dja, ka).start()

    sn_rows = transposed(sn_t)
    sn_f[...] = sn_rows

    def add_planes(b, total):
        for u in range(8):
            j = b * 8 + u
            total = total + wide[j, :tk] * sn_f[pl.ds(j, 1), :]
            total = total + wide[j, tk:] * sn_f[pl.ds(j + half, 1), :]
        return total

    tsum = lax.fori_loop(0, half // 8, add_planes, jnp.zeros((tk, rank), F32))
    ts_loc[...] = tsum.T.reshape(nia * nja, q3, tk)
    ts_in[slot3] = ts_loc[slot3]

    @pl.loop(0, nia * nja - 1)
    def _(t):
        dia, dja = plane_of(t)
        remote(
            ts_loc.at[dia * nja + dja], ts_in.at[slot3], send_sem.at[14], recv_sem.at[14], dia, dja, ka
        ).start()

    second_out[...] = sn_f[...].astype(BF16)
    wait_bytes(gn_in.at[pl.ds(0, nja - 1)], recv_sem.at[13])
    gram_rows = gf_sum[ja] * jnp.sum(gn_in[...], axis=0)
    time_den = exact_product(gram_rows, time_ref[...])
    wait_bytes(ts_in.at[pl.ds(0, nia * nja - 1)], recv_sem.at[14])
    time_num = jnp.sum(ts_in[...], axis=0)
    tn_in[slot3] = (time_t[slot3] * time_num / time_den).astype(BF16)

    @pl.loop(0, nia * nja - 1)
    def _(t):
        dia, dja = plane_of(t)
        remote(
            tn_in.at[slot3], tn_in.at[slot3], send_sem.at[15], recv_sem.at[15], dia, dja, ka
        ).start()

    @pl.loop(0, nia)
    def _(s):
        pair_copy(s).wait_send()

    slab_copy.wait_send()
    gc_copy.wait_send()
    fn_copy.wait_send()
    for place_, ref in (
        (0, ring_in),
        (1, gc_in.at[pl.ds(0, groups - 1)]),
        (2, gs_in.at[pl.ds(0, nja - 1)]),
        (3, gt_in.at[pl.ds(0, nka - 1)]),
        (5, ga_in.at[pl.ds(0, nia - 1)]),
        (6, sum_in.at[pl.ds(0, groups - 1)]),
        (7, fn_in.at[0, pl.ds(0, groups - 1)]),
        (8, gt_wide.at[pl.ds(0, nka - 1)]),
        (10, ps_in.at[pl.ds(0, nia - 1)]),
        (11, pa_in.at[pl.ds(0, nka - 1)]),
        (13, gn_in.at[pl.ds(0, nja - 1)]),
        (14, ts_in.at[pl.ds(0, nia * nja - 1)]),
        (15, tn_in.at[pl.ds(0, nia * nja - 1)]),
        (16, gf_in.at[pl.ds(0, nia - 1)]),
        (17, sn_in.at[pl.ds(0, nia - 1)]),
    ):
        wait_bytes(ref, send_sem.at[place_])

    wait_bytes(tn_in.at[pl.ds(0, nia * nja - 1)], recv_sem.at[15])
    tn_t = tn_in[...].astype(F32).reshape(rank, tk).astype(BF16)
    time_out[...] = transposed(tn_t).astype(BF16)


def hand_out(first, second, time, first_out, second_out, time_out):
    first_out[...] = first[...]
    second_out[...] = second[...]
    time_out[...] = time[...]


def on_device(nia, nja, nka, tensor, matrix, first_factor, second_factor, time_factor, column_factor):
    ti, tj, tk = tensor.shape
    rank = first_factor.shape[1]
    depth = column_factor.shape[0]
    nyh = nja // 2
    slots = nja * nka
    q1, q3 = rank // slots, rank // (nia * nja)
    q4 = nja * q3
    groups = nka * nyh
    half = tj // 2
    V = pltpu.VMEM
    scratch = [
        V((ti, tj, tk), BF16),
        V((half, ti, 2 * tk), BF16),
        V((half, 2 * tk, ti), BF16),
        V((half, 2 * tk, rank), F32),
        V((nia, ti, depth), BF16),
        V((rank, depth), BF16),
        V((nia, 2, groups, q1, ti), F32),
        V((nia, groups, q1, ti), F32),
        V((nia - 1, groups, q1, ti), F32),
        V((ti, rank), F32),
        V((2, groups, q1, ti), F32),
        V((groups, q1, ti), F32),
        V((groups, q1, ti), F32),
        V((groups, q1, ti), F32),
        V((2, groups, q1, rank), F32),
        V((groups, q1, rank), F32),
        V((groups, q1, rank), F32),
        V((groups, q1, rank), F32),
        V((slots, q1, rank), F32),
        V((nja, q1, rank), F32),
        V((slots, q1, rank), F32),
        V((nka, q1, rank), F32),
        V((nka, q4 // q1, q1, rank), F32),
        V((nia, q1, rank), F32),
        V((slots, q1, ti), F32),
        V((nia, q4, tj), F32),
        V((nia * nja, q3, tk), F32),
        V((tj, rank), F32),
        V((tk, rank), F32),
        V((2, groups, q1, ti), BF16),
        V((nia, q4, rank), F32),
        V((nia, q4, rank), F32),
        V((nja, q3, rank), F32),
        V((tj, rank), F32),
        V((nia, q4, tj), F32),
        V((nia, q4, tj), F32),
        V((nka, q4, tj), F32),
        V((nia, q4, tj), BF16),
        V((nja, q3, rank), F32),
        V((nja, q3, rank), F32),
        V((tj, rank), F32),
        V((nia * nja, q3, tk), F32),
        V((nia * nja, q3, tk), F32),
        V((nia * nja, q3, tk), BF16),
        pltpu.SemaphoreType.DMA((nia,)),
        pltpu.SemaphoreType.DMA((ti // 16,)),
        pltpu.SemaphoreType.DMA((nia,)),
        pltpu.SemaphoreType.DMA((nia,)),
        pltpu.SemaphoreType.DMA((18,)),
        pltpu.SemaphoreType.DMA((18,)),
    ]
    in_vmem = pl.BlockSpec(memory_space=pltpu.VMEM)
    in_place = pl.BlockSpec(memory_space=pl.ANY)
    shapes = (
        jax.ShapeDtypeStruct((ti, rank), BF16),
        jax.ShapeDtypeStruct((tj, rank), BF16),
        jax.ShapeDtypeStruct((tk, rank), BF16),
    )
    results = pl.pallas_call(
        functools.partial(kernel, (nia, nja, nka, rank, ti, tj, tk)),
        out_shape=shapes,
        in_specs=[in_place, in_place, in_vmem, in_vmem, in_vmem, in_vmem],
        out_specs=(in_vmem, in_vmem, in_vmem),
        scratch_shapes=scratch,
        compiler_params=pltpu.CompilerParams(
            collective_id=0, has_side_effects=True, vmem_limit_bytes=60 * 1024 * 1024
        ),
        name="factor_round",
    )(tensor, matrix, first_factor, second_factor, time_factor, column_factor)
    return pl.pallas_call(
        hand_out,
        out_shape=shapes,
        in_specs=[in_vmem] * 3,
        out_specs=(in_vmem,) * 3,
        name="hand_out",
    )(*results)


def solution(mesh):
    sizes = (mesh.shape["ia"], mesh.shape["ja"], mesh.shape["ka"])
    return jax.shard_map(
        functools.partial(on_device, *sizes),
        mesh=mesh,
        in_specs=(
            P("ia", "ja", "ka"),
            P(None, ("ia", "ja", "ka")),
            P("ia", None),
            P("ja", None),
            P("ka", None),
            P(("ia", "ja", "ka"), None),
        ),
        out_specs=(P("ia", None), P("ja", None), P("ka", None)),
        check_vma=False,
    )
```
